32 devices in a mesh: lat: 4 (over z), lon: 8 (over y, x, core).
Axes of the slice: x: 2, y: 2, z: 4, core: 2. Of those that a mesh axis runs over, the one named last changes fastest.
Arguments:
- covariance: float32 [4, 4, 128, 128], P('lat', None, 'lon'), may hold values from -6 to 6
- winds: float32 [2, 3, 4, 128], P(None, None, None, 'lon'), may hold values from -0.35 to 0.35
- diffusivity: float32 [4, 128], P(None, 'lon'), may hold values from 0.01 to 0.07
- cutoff: int32 [4], replicated, may hold values from 0 to 1, as said below
Outputs:
- forecast: float32 [4, 4, 128, 128], P('lat', None, 'lon')
The draws below stay inside these ranges and needn't reach their ends.
Inputs may be any that keep to these rules, and one draw needn't show every extreme that they name: Some latitude has cutoff 1 and some other has 0.
All inputs are finite; a program needn't handle non-finite values.
Results may differ from the reference program's by a relative error of at most 0.00002.
Values sent between devices are 32-bit elements; how exact they have to be, the bound alone decides.
No kernel may reach another device: no remote copies, remote signals or barrier semaphores. Data moves between devices by JAX's collectives and lax.ppermute only.
A program may use at most 192 MiB of HBM per device.

```python
import math
import jax
import jax.numpy as jnp
from jax import lax

STEPS = 3
NLAT = 4
NLON = 128
BAND = 1


def draw_cutoff(key, part):
    key_values, key_top, key_low = jax.random.split(key, 3)
    values = jax.random.randint(key_values, (NLAT,), BAND // 4, BAND + 1)
    top_at = jax.random.randint(key_top, (), 0, NLAT)
    low_at = (top_at + 1 + jax.random.randint(key_low, (), 0, NLAT - 1)) % NLAT
    places = jnp.arange(NLAT)
    values = jnp.where(places == top_at, BAND, values)
    values = jnp.where(places == low_at, BAND // 4, values)
    return values.astype(jnp.int32)


def block_levels(key, extent, pieces, low, high):
    level, own = 1.0, jax.random.fold_in(key, 6)
    for axis_at, blocks in pieces:
        heights = jnp.exp(jax.random.uniform(jax.random.fold_in(own, axis_at), (blocks,), jnp.float32, low / len(pieces), high / len(pieces)))
        level = level * jnp.repeat(heights, extent[axis_at] // blocks).reshape([-1 if axis == axis_at else 1 for axis in range(len(extent))])
    return level


def noise(stream_key, extent, width, most, pieces=(), kind=jnp.bfloat16):
    gain = block_levels(stream_key, extent, pieces, -0.22, 0.18) if pieces else 1.0
    result = jax.random.normal(stream_key, extent, jnp.float32) * width * gain
    return jnp.minimum(jnp.maximum(result, -most), most).astype(kind)


def setup_inputs(seed: int = 0) -> dict:
    seeds = jax.random.split(jax.random.key(seed), 5)
    return {
        "covariance": noise(seeds[0], (NLAT, NLAT, NLON, NLON), 1.0, 6.0, ((0, 4), (2, 8)), jnp.float32),
        "winds": jnp.clip(jax.random.uniform(seeds[1], (2, STEPS, NLAT, NLON), jnp.float32, -0.35, 0.35) * block_levels(seeds[1], (2, STEPS, NLAT, NLON), ((3, 8),), -0.4, 0.0), -0.35, 0.35),
        "diffusivity": jnp.clip(jnp.exp(math.log(0.07) - 1.9459102 * jax.random.uniform(seeds[2], (NLAT, NLON), jnp.float32) ** block_levels(seeds[2], (NLAT, NLON), ((1, 8),), -0.2, 0.2)), 0.01, 0.07),
        "cutoff": draw_cutoff(jax.random.fold_in(seeds[4], 71), 0),
    }


def advance(tracer, east_wind, north_wind, spread):
    western = jnp.roll(tracer, 1, axis=1)
    eastern = jnp.roll(tracer, -1, axis=1)
    zeros_row = jnp.zeros_like(tracer[:1])
    southern = jnp.concatenate([zeros_row, tracer[:-1]], axis=0)
    northern = jnp.concatenate([tracer[1:], zeros_row], axis=0)
    east_wind = east_wind[:, :, None]
    north_wind = north_wind[:, :, None]
    spread = spread[:, :, None]
    transport = (jnp.maximum(east_wind, 0.0) * (tracer - western)
                 + jnp.minimum(east_wind, 0.0) * (eastern - tracer)
                 + jnp.maximum(north_wind, 0.0) * (tracer - southern)
                 + jnp.minimum(north_wind, 0.0) * (northern - tracer))
    return tracer - transport + spread * (eastern + western + northern + southern - 4.0 * tracer)


def evolve(tracer, winds, diffusivity):
    for substep in range(STEPS):
        tracer = advance(tracer, winds[0, substep], winds[1, substep], diffusivity)
    return tracer


def reference(covariance, winds, diffusivity, cutoff):
    latitude = jnp.arange(NLAT, dtype=jnp.int32)
    keep_first = jnp.abs(latitude[None, :] - latitude[:, None]) <= cutoff[None, :]
    state_field = jnp.where(keep_first[:, :, None, None], covariance, 0.0)
    state_field = lax.map(lambda lat_row: evolve(lat_row, winds, diffusivity), state_field)
    state_field = jnp.transpose(state_field, (1, 0, 3, 2))
    state_field = lax.map(lambda lat_row: evolve(lat_row, winds, diffusivity), state_field)
    keep_second = jnp.abs(latitude[None, :] - latitude[:, None]) <= cutoff[:, None]
    state_field = jnp.where(keep_second[:, :, None, None], state_field, 0.0)
    return jnp.transpose(state_field, (1, 0, 3, 2))
```

```python
import functools

import jax
import jax.numpy as jnp
from jax import lax
from jax.experimental import pallas as pl
from jax.experimental.pallas import tpu as pltpu
from jax.sharding import PartitionSpec as P

STEPS = 3
FIELDS = 2 * STEPS + 1
VMEM = pl.BlockSpec(memory_space=pltpu.VMEM)
SMEM = pl.BlockSpec(memory_space=pltpu.SMEM)


def shifted(shard, axis, by, wrap):
    size = lax.axis_size(axis)
    pairs = [(i, (i + by) % size) for i in range(size) if wrap or 0 <= i + by < size]
    return lax.ppermute(shard, axis, pairs)


def weights(east_wind, north_wind, spread):
    west = jnp.maximum(east_wind, 0.0) + spread
    east = spread - jnp.minimum(east_wind, 0.0)
    south = jnp.maximum(north_wind, 0.0) + spread
    north = spread - jnp.minimum(north_wind, 0.0)
    return west, east, south, north, 1.0 - (west + east + south + north)


def general(covariance, winds, diffusivity, cutoff):
    row_count, lat_count, lon_local, lon_count = covariance.shape
    blocks = lat_count // row_count
    device_index = lax.axis_index("lat")
    rows = device_index * row_count + jnp.arange(row_count, dtype=jnp.int32)
    lats = jnp.arange(lat_count, dtype=jnp.int32)
    keep = jnp.abs(lats[None, :] - rows[:, None]) <= cutoff[None, :]
    keep = keep[:, :, None, None]
    stacked = jnp.concatenate([winds.reshape(2 * STEPS, lat_count, lon_local), diffusivity[None]])
    everywhere = lax.all_gather(stacked, "lon", axis=2, tiled=True)
    left = shifted(stacked[:, :, -STEPS:], "lon", 1, True)
    right = shifted(stacked[:, :, :STEPS], "lon", -1, True)
    near = jnp.concatenate([left, stacked, right], axis=2)

    field = jnp.where(keep, covariance, 0.0)
    left = shifted(field[:, :, -STEPS:], "lon", 1, True)
    right = shifted(field[:, :, :STEPS], "lon", -1, True)
    field = jnp.concatenate([left, field, right], axis=2)
    for step in range(STEPS):
        width = near.shape[2] - 2 * step
        take = functools.partial(lax.slice_in_dim, start_index=step + 1, limit_index=step + width - 1, axis=1)
        west, east, south, north, own = (
            w[None, :, :, None]
            for w in weights(take(near[step]), take(near[STEPS + step]), take(near[2 * STEPS]))
        )
        center = field[:, :, 1:-1]
        none = jnp.zeros_like(center[:, :1])
        field = (
            own * center
            + west * field[:, :, :-2]
            + east * field[:, :, 2:]
            + south * jnp.concatenate([none, center[:, :-1]], axis=1)
            + north * jnp.concatenate([center[:, 1:], none], axis=1)
        )

    reach = min(-(-STEPS // row_count), blocks - 1)
    halo = min(STEPS, reach * row_count)
    below = [shifted(field, "lat", by, False) for by in range(reach, 0, -1)]
    above = [shifted(field, "lat", -by, False) for by in range(1, reach + 1)]
    window = jnp.concatenate([*below, field, *above])
    window = window[reach * row_count - halo : (reach + 1) * row_count + halo]
    padded = jnp.pad(everywhere, ((0, 0), (halo, halo), (0, 0)))
    local = lax.dynamic_slice_in_dim(padded, device_index * row_count, row_count + 2 * halo, 1)
    for step in range(STEPS):
        west, east, south, north, own = (
            w[:, None, None, :] for w in weights(local[step], local[STEPS + step], local[2 * STEPS])
        )
        none = jnp.zeros_like(window[:1])
        window = (
            own * window
            + west * jnp.roll(window, 1, axis=3)
            + east * jnp.roll(window, -1, axis=3)
            + south * jnp.concatenate([none, window[:-1]])
            + north * jnp.concatenate([window[1:], none])
        )
        inside = device_index * row_count - halo + jnp.arange(window.shape[0])
        inside = (inside >= 0) & (inside < lat_count)
        window = jnp.where(inside[:, None, None, None], window, 0.0)
    return jnp.where(keep, window[halo : halo + row_count], 0.0)


def place():
    lat = lax.axis_index("lat")
    lon = lax.axis_index("lon")
    return lat, lon, lax.rem(lon, 2)


def extra_source(lat, lon, count):
    core = lon % 2
    steps = (4, 5 - 2 * core, 6 + 4 * core, 11 - 6 * core)
    if isinstance(lat, int):
        return (lon + steps[lat]) % count
    step = jnp.where(lat < 2, jnp.where(lat == 0, *steps[:2]), jnp.where(lat == 2, *steps[2:]))
    return lax.rem(lon + step, count)


def prepare_kernel(cutoff, covariance, winds, diffusivity, to_core, to_cross, packed, banded):
    lat, _, core = place()
    lats, width = banded.shape[0], banded.shape[1]
    packed[...] = jnp.zeros_like(packed)
    for step in range(STEPS):
        for kind in range(2):
            at = (kind * STEPS + step) * width
            packed[:, at : at + width] = winds[kind, step]
    packed[:, 2 * STEPS * width : FIELDS * width] = diffusivity[...]
    for i in range(lats):
        keep = jnp.abs(i - lat) <= cutoff[i]
        banded[i] = jnp.where(keep, covariance[0, i], 0.0)
        first, last = banded[i, :STEPS], banded[i, width - STEPS :]
        rows = pl.ds(i * STEPS, STEPS)
        to_core[rows] = jnp.where(core == 0, last, first)
        to_cross[rows] = jnp.where(core == 0, first, last)
    rows = pl.ds(lats * STEPS, lats)
    to_core[rows] = packed[...]
    to_cross[rows] = packed[...]


def first_kernel(banded, packed, from_core, from_cross, extra, own, out_1, out_2, out_3, relay, columns):
    lat, _, core = place()
    lats, width, lon_count = banded.shape
    edge = lats * STEPS
    left = jnp.where(core == 0, from_cross[...], from_core[...])
    right = jnp.where(core == 0, from_core[...], from_cross[...])
    relay[...] = from_cross[edge:]
    columns[...] = jnp.zeros_like(columns)
    columns[0:lats] = packed[...]
    columns[lats : 2 * lats] = left[edge:]
    columns[2 * lats : 3 * lats] = right[edge:]
    turned = columns[...].T

    def spread_of(f, i):
        lo = f * width
        low = turned[lo + width - 8 : lo + width, lats + i : lats + i + 1]
        mid = turned[lo : lo + width, i : i + 1]
        high = turned[lo : lo + 8, 2 * lats + i : 2 * lats + i + 1]
        return jnp.broadcast_to(jnp.concatenate([low, mid, high]), (width + 16, lon_count))

    gap = jnp.zeros((8 - STEPS, lon_count), jnp.float32)
    field = [
        jnp.concatenate(
            [
                gap,
                left[i * STEPS : (i + 1) * STEPS],
                banded[i],
                right[i * STEPS : (i + 1) * STEPS],
                gap,
            ]
        )
        for i in range(lats)
    ]
    diffusion = [spread_of(2 * STEPS, i) for i in range(lats)]
    for step in range(STEPS):
        new = []
        for i in range(lats):
            west, east, south, north, here = weights(
                spread_of(step, i), spread_of(STEPS + step, i), diffusion[i]
            )
            value = here * field[i]
            value += west * pltpu.roll(field[i], 1, 0)
            value += east * pltpu.roll(field[i], width + 15, 0)
            if i > 0:
                value += south * field[i - 1]
            if i < lats - 1:
                value += north * field[i + 1]
            new.append(value)
        field = new
    for i in range(lats):
        own[i] = field[i][8 : 8 + width]
    for by, out in ((1, out_1), (2, out_2), (3, out_3)):
        target = lat ^ by
        for slot in range(3):
            i = jnp.clip(target - 1 + slot, 0, lats - 1)
            out[slot * width : (slot + 1) * width] = own[i]
        out[3 * width :] = extra[...]


def second_kernel(
    cutoff, own, in_1, in_2, in_3, packed, from_core, from_cross, extra, relay, out, field, result
):
    lat, lon, core = place()
    lats, width, lon_count = own.shape
    blocks = lon_count // width
    edge = lats * STEPS
    tall = 3 * width
    cross = lax.rem(lon + blocks - 1 + 2 * core, blocks)
    partner = lon ^ 1
    other = lax.rem(lon + 2 - 4 * core + blocks, blocks)
    pieces = [
        (packed[...], lon),
        (from_core[edge:], partner),
        (from_cross[edge:], cross),
        (relay[...], other),
        (extra[...], extra_source(lat, lon, blocks)),
        (in_1[tall:], extra_source(lat ^ 1, lon, blocks)),
        (in_2[tall:], extra_source(lat ^ 2, lon, blocks)),
        (in_3[tall:], extra_source(lat ^ 3, lon, blocks)),
    ]
    group = lax.broadcasted_iota(jnp.int32, (lats, lon_count), 1) // width
    ready = [(pltpu.roll(piece, at * width, 1), group == at) for piece, at in pieces]
    fields = []
    for f in range(FIELDS):
        total = None
        for piece, mask in ready:
            back = piece if f == 0 else pltpu.roll(piece, lon_count - f * width, 1)
            part = jnp.where(mask, back, 0.0)
            total = part if total is None else total + part
        fields.append(total)

    for slot in range(3):
        i = jnp.clip(lat - 1 + slot, 0, lats - 1)
        field[lat, slot * width : (slot + 1) * width] = own[i]
    for by, block in ((1, in_1), (2, in_2), (3, in_3)):
        field[lat ^ by] = block[:tall]
    values = [field[j] for j in range(lats)]
    for step in range(STEPS):
        coefficients = weights(fields[step], fields[STEPS + step], fields[2 * STEPS])
        new = []
        for j in range(lats):
            west, east, south, north, here = (
                jnp.broadcast_to(w[j : j + 1], (tall, lon_count)) for w in coefficients
            )
            value = here * values[j]
            value += west * pltpu.roll(values[j], 1, 1)
            value += east * pltpu.roll(values[j], lon_count - 1, 1)
            if j > 0:
                value += south * values[j - 1]
            if j < lats - 1:
                value += north * values[j + 1]
            new.append(value)
        values = new
    for j in range(lats):
        result[j] = values[j]
    for i in range(lats):
        slot = i - lat + 1
        keep = (slot >= 0) & (slot <= 2) & (jnp.abs(i - lat) <= cutoff[i])
        at = pl.multiple_of(jnp.clip(slot, 0, 2) * width, width)
        out[0, i] = jnp.where(keep, result[lat, pl.ds(at, width)], 0.0)


def single_row(covariance, winds, diffusivity, cutoff):
    _, lats, width, lon_count = covariance.shape
    count = lax.axis_size("lon")

    def shape(*dims):
        return jax.ShapeDtypeStruct(dims, jnp.float32)

    tall = 3 * width
    edge = shape(lats * STEPS + lats, lon_count)
    wind = shape(lats, lon_count)
    block = shape(lats, width, lon_count)
    message = shape(tall + lats, lon_count)
    to_core, to_cross, packed, banded = pl.pallas_call(
        prepare_kernel,
        out_shape=(edge, edge, wind, block),
        in_specs=[SMEM, VMEM, VMEM, VMEM],
        out_specs=(VMEM,) * 4,
    )(cutoff, covariance, winds, diffusivity)

    pair = [(i, i ^ 1) for i in range(count)]
    odd = [i for i in range(count) if i % 2]
    beyond = [p for i in odd for p in ((i, (i + 1) % count), ((i + 1) % count, i))]
    rows = range(lats)
    fetch = [(l * count + extra_source(l, m, count), l * count + m) for l in rows for m in range(count)]
    from_cross = lax.ppermute(to_cross, "lon", beyond)
    from_core = lax.ppermute(to_core, "lon", pair)
    extra = lax.ppermute(packed, ("lat", "lon"), fetch)

    own, out_1, out_2, out_3, relay = pl.pallas_call(
        first_kernel,
        out_shape=(block, message, message, message, wind),
        in_specs=[VMEM] * 5,
        out_specs=(VMEM,) * 5,
        scratch_shapes=[pltpu.VMEM((lon_count, lon_count), jnp.float32)],
    )(banded, packed, from_core, from_cross, extra)

    in_1, in_2, in_3 = (
        lax.ppermute(out, "lat", [(l, l ^ by) for l in rows])
        for by, out in ((1, out_1), (2, out_2), (3, out_3))
    )
    relay = lax.ppermute(relay, "lon", pair)
    return pl.pallas_call(
        second_kernel,
        out_shape=shape(1, lats, width, lon_count),
        in_specs=[SMEM] + [VMEM] * 9,
        out_specs=VMEM,
        scratch_shapes=[pltpu.VMEM((lats, tall, lon_count), jnp.float32)] * 2,
    )(cutoff, own, in_1, in_2, in_3, packed, from_core, from_cross, extra, relay)


def per_device(covariance, winds, diffusivity, cutoff):
    fits = lax.axis_size("lat") == 4 and lax.axis_size("lon") == 8
    fits = fits and covariance.shape == (1, 4, 16, 128)
    return (single_row if fits else general)(covariance, winds, diffusivity, cutoff)


def solution(mesh):
    in_specs = (P("lat", None, "lon", None), P(None, None, None, "lon"), P(None, "lon"), P())
    out_specs = P("lat", None, "lon", None)
    return jax.shard_map(
        per_device, mesh=mesh, in_specs=in_specs, out_specs=out_specs, check_vma=False
    )
```

```python
import functools

import jax
import jax.numpy as jnp
from jax import lax
from jax.experimental import pallas as pl
from jax.experimental.pallas import tpu as pltpu
from jax.sharding import PartitionSpec as P

STEPS = 3
FIELDS = 2 * STEPS + 1
VMEM = pl.BlockSpec(memory_space=pltpu.VMEM)
SMEM = pl.BlockSpec(memory_space=pltpu.SMEM)


def shifted(shard, axis, by, wrap):
    size = lax.axis_size(axis)
    pairs = [(i, (i + by) % size) for i in range(size) if wrap or 0 <= i + by < size]
    return lax.ppermute(shard, axis, pairs)


def weights(east_wind, north_wind, spread):
    west = jnp.maximum(east_wind, 0.0) + spread
    east = spread - jnp.minimum(east_wind, 0.0)
    south = jnp.maximum(north_wind, 0.0) + spread
    north = spread - jnp.minimum(north_wind, 0.0)
    return west, east, south, north, 1.0 - (west + east + south + north)


def general(covariance, winds, diffusivity, cutoff):
    row_count, lat_count, lon_local, lon_count = covariance.shape
    blocks = lat_count // row_count
    device_index = lax.axis_index("lat")
    rows = device_index * row_count + jnp.arange(row_count, dtype=jnp.int32)
    lats = jnp.arange(lat_count, dtype=jnp.int32)
    keep = jnp.abs(lats[None, :] - rows[:, None]) <= cutoff[None, :]
    keep = keep[:, :, None, None]
    stacked = jnp.concatenate([winds.reshape(2 * STEPS, lat_count, lon_local), diffusivity[None]])
    everywhere = lax.all_gather(stacked, "lon", axis=2, tiled=True)
    left = shifted(stacked[:, :, -STEPS:], "lon", 1, True)
    right = shifted(stacked[:, :, :STEPS], "lon", -1, True)
    near = jnp.concatenate([left, stacked, right], axis=2)

    field = jnp.where(keep, covariance, 0.0)
    left = shifted(field[:, :, -STEPS:], "lon", 1, True)
    right = shifted(field[:, :, :STEPS], "lon", -1, True)
    field = jnp.concatenate([left, field, right], axis=2)
    for step in range(STEPS):
        width = near.shape[2] - 2 * step
        take = functools.partial(lax.slice_in_dim, start_index=step + 1, limit_index=step + width - 1, axis=1)
        west, east, south, north, own = (
            w[None, :, :, None]
            for w in weights(take(near[step]), take(near[STEPS + step]), take(near[2 * STEPS]))
        )
        center = field[:, :, 1:-1]
        none = jnp.zeros_like(center[:, :1])
        field = (
            own * center
            + west * field[:, :, :-2]
            + east * field[:, :, 2:]
            + south * jnp.concatenate([none, center[:, :-1]], axis=1)
            + north * jnp.concatenate([center[:, 1:], none], axis=1)
        )

    reach = min(-(-STEPS // row_count), blocks - 1)
    halo = min(STEPS, reach * row_count)
    below = [shifted(field, "lat", by, False) for by in range(reach, 0, -1)]
    above = [shifted(field, "lat", -by, False) for by in range(1, reach + 1)]
    window = jnp.concatenate([*below, field, *above])
    window = window[reach * row_count - halo : (reach + 1) * row_count + halo]
    padded = jnp.pad(everywhere, ((0, 0), (halo, halo), (0, 0)))
    local = lax.dynamic_slice_in_dim(padded, device_index * row_count, row_count + 2 * halo, 1)
    for step in range(STEPS):
        west, east, south, north, own = (
            w[:, None, None, :] for w in weights(local[step], local[STEPS + step], local[2 * STEPS])
        )
        none = jnp.zeros_like(window[:1])
        window = (
            own * window
            + west * jnp.roll(window, 1, axis=3)
            + east * jnp.roll(window, -1, axis=3)
            + south * jnp.concatenate([none, window[:-1]])
            + north * jnp.concatenate([window[1:], none])
        )
        inside = device_index * row_count - halo + jnp.arange(window.shape[0])
        inside = (inside >= 0) & (inside < lat_count)
        window = jnp.where(inside[:, None, None, None], window, 0.0)
    return jnp.where(keep, window[halo : halo + row_count], 0.0)


def place():
    lat = lax.axis_index("lat")
    lon = lax.axis_index("lon")
    return lat, lon, lax.rem(lon, 2)


def extra_source(lat, lon, count):
    core = lon % 2
    steps = (4, 5 - 2 * core, 6 + 4 * core, 11 - 6 * core)
    if isinstance(lat, int):
        return (lon + steps[lat]) % count
    step = jnp.where(lat < 2, jnp.where(lat == 0, *steps[:2]), jnp.where(lat == 2, *steps[2:]))
    return lax.rem(lon + step, count)


def prepare_kernel(cutoff, covariance, winds, diffusivity, to_core, to_cross, packed, banded):
    lat, _, core = place()
    lats, width = banded.shape[0], banded.shape[1]
    packed[...] = jnp.zeros_like(packed)
    for step in range(STEPS):
        for kind in range(2):
            at = (kind * STEPS + step) * width
            packed[:, at : at + width] = winds[kind, step]
    packed[:, 2 * STEPS * width : FIELDS * width] = diffusivity[...]
    for i in range(lats):
        keep = jnp.abs(i - lat) <= cutoff[i]
        banded[i] = jnp.where(keep, covariance[0, i], 0.0)
        first, last = banded[i, :STEPS], banded[i, width - STEPS :]
        rows = pl.ds(i * STEPS, STEPS)
        to_core[rows] = jnp.where(core == 0, last, first)
        to_cross[rows] = jnp.where(core == 0, first, last)
    rows = pl.ds(lats * STEPS, lats)
    to_core[rows] = packed[...]
    to_cross[rows] = packed[...]


def first_kernel(banded, packed, from_core, from_cross, extra, own, out_1, out_2, out_3, relay, columns):
    lat, _, core = place()
    lats, width, lon_count = banded.shape
    edge = lats * STEPS
    left = jnp.where(core == 0, from_cross[...], from_core[...])
    right = jnp.where(core == 0, from_core[...], from_cross[...])
    relay[...] = from_cross[edge:]
    columns[...] = jnp.zeros_like(columns)
    columns[0:lats] = packed[...]
    columns[lats : 2 * lats] = left[edge:]
    columns[2 * lats : 3 * lats] = right[edge:]
    turned = columns[...].T

    def spread_of(f, i):
        lo = f * width
        low = turned[lo + width - 8 : lo + width, lats + i : lats + i + 1]
        mid = turned[lo : lo + width, i : i + 1]
        high = turned[lo : lo + 8, 2 * lats + i : 2 * lats + i + 1]
        return jnp.broadcast_to(jnp.concatenate([low, mid, high]), (width + 16, lon_count))

    gap = jnp.zeros((8 - STEPS, lon_count), jnp.float32)
    field = [
        jnp.concatenate(
            [
                gap,
                left[i * STEPS : (i + 1) * STEPS],
                banded[i],
                right[i * STEPS : (i + 1) * STEPS],
                gap,
            ]
        )
        for i in range(lats)
    ]
    diffusion = [spread_of(2 * STEPS, i) for i in range(lats)]
    for step in range(STEPS):
        new = []
        for i in range(lats):
            west, east, south, north, here = weights(
                spread_of(step, i), spread_of(STEPS + step, i), diffusion[i]
            )
            value = here * field[i]
            value += west * pltpu.roll(field[i], 1, 0)
            value += east * pltpu.roll(field[i], width + 15, 0)
            if i > 0:
                value += south * field[i - 1]
            if i < lats - 1:
                value += north * field[i + 1]
            new.append(value)
        field = new
    for i in range(lats):
        own[i] = field[i][8 : 8 + width]
    for by, out in ((1, out_1), (2, out_2), (3, out_3)):
        target = lat ^ by
        for slot in range(3):
            i = jnp.clip(target - 1 + slot, 0, lats - 1)
            out[slot * width : (slot + 1) * width] = own[i]
        out[3 * width :] = extra[...]


def second_kernel(
    cutoff, own, in_1, in_2, in_3, packed, from_core, from_cross, extra, relay, out, field, result
):
    lat, lon, core = place()
    lats, width, lon_count = own.shape
    blocks = lon_count // width
    edge = lats * STEPS
    tall = 3 * width
    cross = lax.rem(lon + blocks - 1 + 2 * core, blocks)
    partner = lon ^ 1
    other = lax.rem(lon + 2 - 4 * core + blocks, blocks)
    pieces = [
        (packed[...], lon),
        (from_core[edge:], partner),
        (from_cross[edge:], cross),
        (relay[...], other),
        (extra[...], extra_source(lat, lon, blocks)),
        (in_1[tall:], extra_source(lat ^ 1, lon, blocks)),
        (in_2[tall:], extra_source(lat ^ 2, lon, blocks)),
        (in_3[tall:], extra_source(lat ^ 3, lon, blocks)),
    ]
    group = lax.broadcasted_iota(jnp.int32, (lats, lon_count), 1) // width
    ready = [(pltpu.roll(piece, at * width, 1), group == at) for piece, at in pieces]
    fields = []
    for f in range(FIELDS):
        total = None
        for piece, mask in ready:
            back = piece if f == 0 else pltpu.roll(piece, lon_count - f * width, 1)
            part = jnp.where(mask, back, 0.0)
            total = part if total is None else total + part
        fields.append(total)

    for slot in range(3):
        i = jnp.clip(lat - 1 + slot, 0, lats - 1)
        field[lat, slot * width : (slot + 1) * width] = own[i]
    for by, block in ((1, in_1), (2, in_2), (3, in_3)):
        field[lat ^ by] = block[:tall]
    values = [field[j] for j in range(lats)]
    for step in range(STEPS):
        coefficients = weights(fields[step], fields[STEPS + step], fields[2 * STEPS])
        new = []
        for j in range(lats):
            west, east, south, north, here = (
                jnp.broadcast_to(w[j : j + 1], (tall, lon_count)) for w in coefficients
            )
            value = here * values[j]
            value += west * pltpu.roll(values[j], 1, 1)
            value += east * pltpu.roll(values[j], lon_count - 1, 1)
            if j > 0:
                value += south * values[j - 1]
            if j < lats - 1:
                value += north * values[j + 1]
            new.append(value)
        values = new
    for j in range(lats):
        result[j] = values[j]
    for i in range(lats):
        slot = i - lat + 1
        keep = (slot >= 0) & (slot <= 2) & (jnp.abs(i - lat) <= cutoff[i])
        at = pl.multiple_of(jnp.clip(slot, 0, 2) * width, width)
        out[0, i] = jnp.where(keep, result[lat, pl.ds(at, width)], 0.0)


def on_chip(*arrays):
    return [pltpu.with_memory_space_constraint(array, pltpu.VMEM) for array in arrays]


def single_row(covariance, winds, diffusivity, cutoff):
    _, lats, width, lon_count = covariance.shape
    count = lax.axis_size("lon")

    def shape(*dims):
        return pltpu.VMEM(dims, jnp.float32)

    tall = 3 * width
    edge = shape(lats * STEPS + lats, lon_count)
    wind = shape(lats, lon_count)
    block = shape(lats, width, lon_count)
    message = shape(tall + lats, lon_count)
    to_core, to_cross, packed, banded = pl.pallas_call(
        prepare_kernel,
        out_shape=(edge, edge, wind, block),
        in_specs=[SMEM, VMEM, VMEM, VMEM],
        out_specs=(VMEM,) * 4,
    )(cutoff, covariance, winds, diffusivity)

    pair = [(i, i ^ 1) for i in range(count)]
    odd = [i for i in range(count) if i % 2]
    beyond = [p for i in odd for p in ((i, (i + 1) % count), ((i + 1) % count, i))]
    rows = range(lats)
    fetch = [(l * count + extra_source(l, m, count), l * count + m) for l in rows for m in range(count)]
    from_cross = lax.ppermute(to_cross, "lon", beyond)
    from_core = lax.ppermute(to_core, "lon", pair)
    extra = lax.ppermute(packed, ("lat", "lon"), fetch)

    own, out_1, out_2, out_3, relay = pl.pallas_call(
        first_kernel,
        out_shape=(block, message, message, message, wind),
        in_specs=[VMEM] * 5,
        out_specs=(VMEM,) * 5,
        scratch_shapes=[pltpu.VMEM((lon_count, lon_count), jnp.float32)],
    )(*on_chip(banded, packed, from_core, from_cross, extra))

    in_1, in_2, in_3 = (
        lax.ppermute(out, "lat", [(l, l ^ by) for l in rows])
        for by, out in ((1, out_1), (2, out_2), (3, out_3))
    )
    relay = lax.ppermute(relay, "lon", pair)
    return pl.pallas_call(
        second_kernel,
        out_shape=jax.ShapeDtypeStruct(covariance.shape, jnp.float32),
        in_specs=[SMEM] + [VMEM] * 9,
        out_specs=VMEM,
        scratch_shapes=[pltpu.VMEM((lats, tall, lon_count), jnp.float32)] * 2,
    )(cutoff, *on_chip(own, in_1, in_2, in_3, packed, from_core, from_cross, extra, relay))


def per_device(covariance, winds, diffusivity, cutoff):
    fits = lax.axis_size("lat") == 4 and lax.axis_size("lon") == 8
    fits = fits and covariance.shape == (1, 4, 16, 128)
    return (single_row if fits else general)(covariance, winds, diffusivity, cutoff)


def solution(mesh):
    in_specs = (P("lat", None, "lon", None), P(None, None, None, "lon"), P(None, "lon"), P())
    out_specs = P("lat", None, "lon", None)
    return jax.shard_map(
        per_device, mesh=mesh, in_specs=in_specs, out_specs=out_specs, check_vma=False
    )
```

```python
import functools

import jax
import jax.numpy as jnp
from jax import lax
from jax.experimental import pallas as pl
from jax.experimental.pallas import tpu as pltpu
from jax.sharding import PartitionSpec as P

STEPS = 3
FIELDS = 2 * STEPS + 1
VMEM = pl.BlockSpec(memory_space=pltpu.VMEM)
SMEM = pl.BlockSpec(memory_space=pltpu.SMEM)


def shifted(shard, axis, by, wrap):
    size = lax.axis_size(axis)
    pairs = [(i, (i + by) % size) for i in range(size) if wrap or 0 <= i + by < size]
    return lax.ppermute(shard, axis, pairs)


def weights(east_wind, north_wind, spread):
    west = jnp.maximum(east_wind, 0.0) + spread
    east = spread - jnp.minimum(east_wind, 0.0)
    south = jnp.maximum(north_wind, 0.0) + spread
    north = spread - jnp.minimum(north_wind, 0.0)
    return west, east, south, north, 1.0 - (west + east + south + north)


def general(covariance, winds, diffusivity, cutoff):
    row_count, lat_count, lon_local, _ = covariance.shape
    blocks = lat_count // row_count
    device_index = lax.axis_index("lat")
    rows = device_index * row_count + jnp.arange(row_count, dtype=jnp.int32)
    lats = jnp.arange(lat_count, dtype=jnp.int32)
    keep = jnp.abs(lats[None, :] - rows[:, None]) <= cutoff[None, :]
    keep = keep[:, :, None, None]
    stacked = jnp.concatenate([winds.reshape(2 * STEPS, lat_count, lon_local), diffusivity[None]])
    everywhere = lax.all_gather(stacked, "lon", axis=2, tiled=True)
    left = shifted(stacked[:, :, -STEPS:], "lon", 1, True)
    right = shifted(stacked[:, :, :STEPS], "lon", -1, True)
    near = jnp.concatenate([left, stacked, right], axis=2)

    field = jnp.where(keep, covariance, 0.0)
    left = shifted(field[:, :, -STEPS:], "lon", 1, True)
    right = shifted(field[:, :, :STEPS], "lon", -1, True)
    field = jnp.concatenate([left, field, right], axis=2)
    for step in range(STEPS):
        width = near.shape[2] - 2 * step
        take = functools.partial(lax.slice_in_dim, start_index=step + 1, limit_index=step + width - 1, axis=1)
        west, east, south, north, own = (
            w[None, :, :, None]
            for w in weights(take(near[step]), take(near[STEPS + step]), take(near[2 * STEPS]))
        )
        center = field[:, :, 1:-1]
        none = jnp.zeros_like(center[:, :1])
        field = (
            own * center
            + west * field[:, :, :-2]
            + east * field[:, :, 2:]
            + south * jnp.concatenate([none, center[:, :-1]], axis=1)
            + north * jnp.concatenate([center[:, 1:], none], axis=1)
        )

    reach = min(-(-STEPS // row_count), blocks - 1)
    halo = min(STEPS, reach * row_count)
    below = [shifted(field, "lat", by, False) for by in range(reach, 0, -1)]
    above = [shifted(field, "lat", -by, False) for by in range(1, reach + 1)]
    window = jnp.concatenate([*below, field, *above])
    window = window[reach * row_count - halo : (reach + 1) * row_count + halo]
    padded = jnp.pad(everywhere, ((0, 0), (halo, halo), (0, 0)))
    local = lax.dynamic_slice_in_dim(padded, device_index * row_count, row_count + 2 * halo, 1)
    for step in range(STEPS):
        west, east, south, north, own = (
            w[:, None, None, :] for w in weights(local[step], local[STEPS + step], local[2 * STEPS])
        )
        none = jnp.zeros_like(window[:1])
        window = (
            own * window
            + west * jnp.roll(window, 1, axis=3)
            + east * jnp.roll(window, -1, axis=3)
            + south * jnp.concatenate([none, window[:-1]])
            + north * jnp.concatenate([window[1:], none])
        )
        inside = device_index * row_count - halo + jnp.arange(window.shape[0])
        inside = (inside >= 0) & (inside < lat_count)
        window = jnp.where(inside[:, None, None, None], window, 0.0)
    return jnp.where(keep, window[halo : halo + row_count], 0.0)


def place():
    lon = lax.axis_index("lon")
    return lax.axis_index("lat"), lon, lax.rem(lon, 2)


def prepare_kernel(cutoff, covariance, winds, diffusivity, to_core, to_cross, packed, banded, kept):
    lat, _, core = place()
    lats, width, lon_count = banded.shape
    packed[...] = jnp.zeros_like(packed)
    for step in range(STEPS):
        for kind in range(2):
            at = (kind * STEPS + step) * width
            packed[:, at : at + width] = winds[kind, step]
    packed[:, 2 * STEPS * width : FIELDS * width] = diffusivity[...]
    for i in range(lats):
        keep = jnp.abs(i - lat) <= cutoff[i]
        kept[i : i + 1] = jnp.full((1, lon_count), jnp.where(keep, 1.0, 0.0), jnp.float32)
        banded[i] = jnp.where(keep, covariance[0, i], 0.0)
        first, last = banded[i, :STEPS], banded[i, width - STEPS :]
        rows = pl.ds(i * STEPS, STEPS)
        to_core[rows] = jnp.where(core == 0, last, first)
        to_cross[rows] = jnp.where(core == 0, first, last)
    rows = pl.ds(lats * STEPS, lats)
    to_core[rows] = packed[...]
    to_cross[rows] = packed[...]


def turn(columns, pieces):
    columns[...] = jnp.zeros_like(columns)
    for at, piece in enumerate(pieces):
        columns[at * piece.shape[0] : (at + 1) * piece.shape[0]] = piece
    return columns[...].T


def middle_kernel(packed, middle, columns):
    lats, lon_count = packed.shape
    width = middle.shape[3]
    turned = turn(columns, [packed[...]])

    def column(f, i):
        return jnp.broadcast_to(turned[f * width : (f + 1) * width, i : i + 1], (width, lon_count))

    for i in range(lats):
        spread = column(2 * STEPS, i)
        for step in range(STEPS):
            found = weights(column(step, i), column(STEPS + step, i), spread)
            for at, weight in enumerate(found):
                middle[step, i, at] = weight


def first_kernel(banded, middle, from_core, from_cross, out_0, out_1, out_2, out_3, columns, done):
    lat, _, core = place()
    lats, width, lon_count = banded.shape
    edge = lats * STEPS
    left = jnp.where(core == 0, from_cross[...], from_core[...])
    right = jnp.where(core == 0, from_core[...], from_cross[...])
    turned = turn(columns, [left[edge:], right[edge:]])

    def column(f, i):
        low = turned[(f + 1) * width - 8 : (f + 1) * width, i : i + 1]
        high = turned[f * width : f * width + 8, lats + i : lats + i + 1]
        return jnp.broadcast_to(jnp.concatenate([low, high]), (16, lon_count))

    gap = jnp.zeros((8 - STEPS, lon_count), jnp.float32)
    field = []
    for i in range(lats):
        rows = slice(i * STEPS, (i + 1) * STEPS)
        field.append(jnp.concatenate([gap, left[rows], banded[i], right[rows], gap]))
    spread = [column(2 * STEPS, i) for i in range(lats)]
    for step in range(STEPS):
        new = []
        for i in range(lats):
            outer = weights(column(step, i), column(STEPS + step, i), spread[i])
            west, east, south, north, here = (
                jnp.concatenate([w[:8], middle[step, i, at], w[8:]]) for at, w in enumerate(outer)
            )
            value = here * field[i]
            value += west * pltpu.roll(field[i], 1, 0)
            value += east * pltpu.roll(field[i], width + 15, 0)
            if i > 0:
                value += south * field[i - 1]
            if i < lats - 1:
                value += north * field[i + 1]
            new.append(value)
        field = new
    for i in range(lats):
        done[i] = field[i][8 : 8 + width].reshape(done.shape[1:])
    tiles = width // 8
    for by, out in enumerate((out_0, out_1, out_2, out_3)):
        for slot in range(3):
            i = jnp.clip((lat ^ by) - 1 + slot, 0, lats - 1)
            out[slot * tiles : (slot + 1) * tiles] = done[i]


def assemble_kernel(packed, from_core, from_cross, far, second, relay, ready):
    lat, lon, core = place()
    lats, lon_count = packed.shape
    edge = lats * STEPS
    width = lon_count // lax.axis_size("lon")
    blocks = lon_count // width
    way = 2 * core - 1
    partner = lon ^ 1
    pieces = [
        (packed[...], lon),
        (from_core[edge:], partner),
        (from_cross[edge:], lon + way),
        (far[...], lon + 4),
        (second[...], lon + 2 * way),
        (relay[:lats], partner - way),
        (relay[lats : 2 * lats], partner + 4),
        (relay[2 * lats :], partner - 2 * way),
    ]
    group = lax.broadcasted_iota(jnp.int32, (lats, lon_count), 1) // width
    turned = []
    for piece, at in pieces:
        at = lax.rem(at + blocks, blocks)
        turned.append((pltpu.roll(piece, at * width, 1), group == at))
    fields = []
    for f in range(FIELDS):
        total = None
        for piece, mask in turned:
            back = piece if f == 0 else pltpu.roll(piece, lon_count - f * width, 1)
            part = jnp.where(mask, back, 0.0)
            total = part if total is None else total + part
        fields.append(total)
    for step in range(STEPS):
        west, east, south, north, here = weights(
            fields[step], fields[STEPS + step], fields[2 * STEPS]
        )
        for row in range(lats):
            near = north if row % 2 == 0 else south
            over = north if row == 1 else south
            for at, weight in enumerate((west, east, near, over, here)):
                line = weight[row : row + 1]
                if at == 3 and row in (0, 3):
                    line = jnp.zeros_like(line)
                ready[step, at, lat ^ row] = jnp.broadcast_to(line, (8, lon_count))


def second_kernel(ready, kept, in_0, in_1, in_2, in_3, out, result):
    lat, _, _ = place()
    lon_count = kept.shape[1]
    values = [block[...] for block in (in_0, in_1, in_2, in_3)]
    for step, slots in enumerate(((0, 1, 2, 3), (0, 1, 3), (0,))):
        new = list(values)
        for s in slots:
            west, east, near, over, here = (ready[step, at, s][None] for at in range(5))
            value = here * values[s] + near * values[s ^ 1] + over * values[s ^ 3]
            value += west * pltpu.roll(values[s], 1, 2)
            value += east * pltpu.roll(values[s], lon_count - 1, 2)
            new[s] = value
        values = new
    result[...] = values[0].reshape(result.shape)
    for i in range(out.shape[1]):
        slot = i - lat + 1
        inside = (slot >= 0) & (slot <= 2)
        keep = (kept[i : i + 1] > 0.0) & inside
        out[0, i] = jnp.where(keep, result[jnp.clip(slot, 0, 2)], 0.0)


def on_chip(*arrays):
    return [pltpu.with_memory_space_constraint(array, pltpu.VMEM) for array in arrays]


def call(kernel, out_shape, scratch_shapes, *arrays):
    return pl.pallas_call(
        kernel,
        out_shape=out_shape,
        in_specs=[VMEM] * len(arrays),
        out_specs=(VMEM,) * len(out_shape) if isinstance(out_shape, tuple) else VMEM,
        scratch_shapes=scratch_shapes,
    )(*on_chip(*arrays))


def single_row(covariance, winds, diffusivity, cutoff):
    _, lats, width, lon_count = covariance.shape
    count = lax.axis_size("lon")

    def shape(*dims):
        return pltpu.VMEM(dims, jnp.float32)

    edge = shape(lats * STEPS + lats, lon_count)
    wind = shape(lats, lon_count)
    tiles = width // 8
    message = shape(3 * tiles, 8, lon_count)
    square = shape(lon_count, lon_count)
    to_core, to_cross, packed, banded, kept = pl.pallas_call(
        prepare_kernel,
        out_shape=(edge, edge, wind, shape(lats, width, lon_count), wind),
        in_specs=[SMEM, VMEM, VMEM, VMEM],
        out_specs=(VMEM,) * 5,
    )(cutoff, covariance, winds, diffusivity)

    lons = range(count)
    pair = [(m, m ^ 1) for m in lons]
    way = [2 * (m % 2) - 1 for m in lons]
    from_cross = lax.ppermute(to_cross, "lon", [((m + way[m]) % count, m) for m in lons])
    from_core = lax.ppermute(to_core, "lon", pair)
    far = lax.ppermute(packed, "lon", [((m + 4) % count, m) for m in lons])
    second = lax.ppermute(packed, "lon", [((m + 2 * way[m]) % count, m) for m in lons])
    middle = call(middle_kernel, shape(STEPS, lats, 5, width, lon_count), [square], packed)

    outs = call(
        first_kernel,
        (message,) * 4,
        [square, shape(lats, tiles, 8, lon_count)],
        banded,
        middle,
        from_core,
        from_cross,
    )
    ins = [outs[0]]
    for by in (1, 2, 3):
        ins.append(lax.ppermute(outs[by], "lat", [(l, l ^ by) for l in range(lats)]))
    winds_here = jnp.concatenate([from_cross[lats * STEPS :], far, second])
    relay = lax.ppermute(winds_here, "lon", pair)
    ready = call(
        assemble_kernel,
        shape(STEPS, 5, lats, 8, lon_count),
        [],
        packed,
        from_core,
        from_cross,
        far,
        second,
        relay,
    )
    return call(
        second_kernel,
        jax.ShapeDtypeStruct(covariance.shape, jnp.float32),
        [shape(3, width, lon_count)],
        ready,
        kept,
        *ins,
    )


def per_device(covariance, winds, diffusivity, cutoff):
    fits = lax.axis_size("lat") == 4 and lax.axis_size("lon") == 8
    fits = fits and covariance.shape == (1, 4, 16, 128)
    return (single_row if fits else general)(covariance, winds, diffusivity, cutoff)


def solution(mesh):
    in_specs = (P("lat", None, "lon", None), P(None, None, None, "lon"), P(None, "lon"), P())
    out_specs = P("lat", None, "lon", None)
    return jax.shard_map(
        per_device, mesh=mesh, in_specs=in_specs, out_specs=out_specs, check_vma=False
    )
```

```python
import functools

import jax
import jax.numpy as jnp
from jax import lax
from jax.experimental import pallas as pl
from jax.experimental.pallas import tpu as pltpu
from jax.sharding import PartitionSpec as P

STEPS = 3
FIELDS = 2 * STEPS + 1
TARGETS = ((2, 3, 1, 0), (3, 2, 0, 1), (1, 0, 3, 2))
SOURCES = tuple(tuple(to.index(row) for row in range(len(to))) for to in TARGETS)
VMEM = pl.BlockSpec(memory_space=pltpu.VMEM)
SMEM = pl.BlockSpec(memory_space=pltpu.SMEM)


def shifted(shard, axis, by, wrap):
    size = lax.axis_size(axis)
    pairs = [(i, (i + by) % size) for i in range(size) if wrap or 0 <= i + by < size]
    return lax.ppermute(shard, axis, pairs)


def weights(east_wind, north_wind, spread):
    west = jnp.maximum(east_wind, 0.0) + spread
    east = spread - jnp.minimum(east_wind, 0.0)
    south = jnp.maximum(north_wind, 0.0) + spread
    north = spread - jnp.minimum(north_wind, 0.0)
    return west, east, south, north, 1.0 - (west + east + south + north)


def general(covariance, winds, diffusivity, cutoff):
    row_count, lat_count, lon_local, _ = covariance.shape
    blocks = lat_count // row_count
    device_index = lax.axis_index("lat")
    rows = device_index * row_count + jnp.arange(row_count, dtype=jnp.int32)
    lats = jnp.arange(lat_count, dtype=jnp.int32)
    keep = jnp.abs(lats[None, :] - rows[:, None]) <= cutoff[None, :]
    keep = keep[:, :, None, None]
    stacked = jnp.concatenate([winds.reshape(2 * STEPS, lat_count, lon_local), diffusivity[None]])
    everywhere = lax.all_gather(stacked, "lon", axis=2, tiled=True)
    left = shifted(stacked[:, :, -STEPS:], "lon", 1, True)
    right = shifted(stacked[:, :, :STEPS], "lon", -1, True)
    near = jnp.concatenate([left, stacked, right], axis=2)

    field = jnp.where(keep, covariance, 0.0)
    left = shifted(field[:, :, -STEPS:], "lon", 1, True)
    right = shifted(field[:, :, :STEPS], "lon", -1, True)
    field = jnp.concatenate([left, field, right], axis=2)
    for step in range(STEPS):
        width = near.shape[2] - 2 * step
        take = functools.partial(lax.slice_in_dim, start_index=step + 1, limit_index=step + width - 1, axis=1)
        west, east, south, north, own = (
            w[None, :, :, None]
            for w in weights(take(near[step]), take(near[STEPS + step]), take(near[2 * STEPS]))
        )
        center = field[:, :, 1:-1]
        none = jnp.zeros_like(center[:, :1])
        field = (
            own * center
            + west * field[:, :, :-2]
            + east * field[:, :, 2:]
            + south * jnp.concatenate([none, center[:, :-1]], axis=1)
            + north * jnp.concatenate([center[:, 1:], none], axis=1)
        )

    reach = min(-(-STEPS // row_count), blocks - 1)
    halo = min(STEPS, reach * row_count)
    below = [shifted(field, "lat", by, False) for by in range(reach, 0, -1)]
    above = [shifted(field, "lat", -by, False) for by in range(1, reach + 1)]
    window = jnp.concatenate([*below, field, *above])
    window = window[reach * row_count - halo : (reach + 1) * row_count + halo]
    padded = jnp.pad(everywhere, ((0, 0), (halo, halo), (0, 0)))
    local = lax.dynamic_slice_in_dim(padded, device_index * row_count, row_count + 2 * halo, 1)
    for step in range(STEPS):
        west, east, south, north, own = (
            w[:, None, None, :] for w in weights(local[step], local[STEPS + step], local[2 * STEPS])
        )
        none = jnp.zeros_like(window[:1])
        window = (
            own * window
            + west * jnp.roll(window, 1, axis=3)
            + east * jnp.roll(window, -1, axis=3)
            + south * jnp.concatenate([none, window[:-1]])
            + north * jnp.concatenate([window[1:], none])
        )
        inside = device_index * row_count - halo + jnp.arange(window.shape[0])
        inside = (inside >= 0) & (inside < lat_count)
        window = jnp.where(inside[:, None, None, None], window, 0.0)
    return jnp.where(keep, window[halo : halo + row_count], 0.0)


def place():
    lon = lax.axis_index("lon")
    return lax.axis_index("lat"), lon, lax.rem(lon, 2)


def entry(table, at):
    found = table[0]
    for index in range(1, len(table)):
        found = jnp.where(at == index, table[index], found)
    return found


def prepare_kernel(cutoff, covariance, winds, diffusivity, to_core, to_cross, packed, banded, kept):
    lat, _, core = place()
    lats, width, lon_count = banded.shape
    packed[...] = jnp.zeros_like(packed)
    for step in range(STEPS):
        for kind in range(2):
            at = (kind * STEPS + step) * width
            packed[:, at : at + width] = winds[kind, step]
    packed[:, 2 * STEPS * width : FIELDS * width] = diffusivity[...]
    for i in range(lats):
        keep = jnp.abs(i - lat) <= cutoff[i]
        kept[i : i + 1] = jnp.full((1, lon_count), jnp.where(keep, 1.0, 0.0), jnp.float32)
        banded[i] = jnp.where(keep, covariance[0, i], 0.0)
        first, last = banded[i, :STEPS], banded[i, width - STEPS :]
        rows = pl.ds(i * STEPS, STEPS)
        to_core[rows] = jnp.where(core == 0, last, first)
        to_cross[rows] = jnp.where(core == 0, first, last)
    rows = pl.ds(lats * STEPS, lats)
    to_core[rows] = packed[...]
    to_cross[rows] = packed[...]


def turn(columns, pieces):
    columns[...] = jnp.zeros_like(columns)
    for at, piece in enumerate(pieces):
        columns[at * piece.shape[0] : (at + 1) * piece.shape[0]] = piece
    return columns[...].T


def middle_kernel(packed, middle, columns):
    lats, lon_count = packed.shape
    width = middle.shape[3]
    turned = turn(columns, [packed[...]])

    def column(f, i):
        return jnp.broadcast_to(turned[f * width : (f + 1) * width, i : i + 1], (width, lon_count))

    for i in range(lats):
        spread = column(2 * STEPS, i)
        for step in range(STEPS):
            found = weights(column(step, i), column(STEPS + step, i), spread)
            for at, weight in enumerate(found):
                middle[step, i, at] = weight


def first_kernel(banded, middle, from_core, from_cross, out_0, out_1, out_2, out_3, columns, done):
    lat, _, core = place()
    lats, width, lon_count = banded.shape
    edge = lats * STEPS
    left = jnp.where(core == 0, from_cross[...], from_core[...])
    right = jnp.where(core == 0, from_core[...], from_cross[...])
    turned = turn(columns, [left[edge:], right[edge:]])

    def column(f, i):
        low = turned[(f + 1) * width - 8 : (f + 1) * width, i : i + 1]
        high = turned[f * width : f * width + 8, lats + i : lats + i + 1]
        return jnp.broadcast_to(jnp.concatenate([low, high]), (16, lon_count))

    gap = jnp.zeros((8 - STEPS, lon_count), jnp.float32)
    field = []
    for i in range(lats):
        rows = slice(i * STEPS, (i + 1) * STEPS)
        field.append(jnp.concatenate([gap, left[rows], banded[i], right[rows], gap]))
    spread = [column(2 * STEPS, i) for i in range(lats)]
    for step in range(STEPS):
        new = []
        for i in range(lats):
            outer = weights(column(step, i), column(STEPS + step, i), spread[i])
            west, east, south, north, here = (
                jnp.concatenate([w[:8], middle[step, i, at], w[8:]]) for at, w in enumerate(outer)
            )
            value = here * field[i]
            value += west * pltpu.roll(field[i], 1, 0)
            value += east * pltpu.roll(field[i], width + 15, 0)
            if i > 0:
                value += south * field[i - 1]
            if i < lats - 1:
                value += north * field[i + 1]
            new.append(value)
        field = new
    for i in range(lats):
        done[i] = field[i][8 : 8 + width].reshape(done.shape[1:])
    tiles = width // 8
    targets = [lat] + [entry(to, lat) for to in TARGETS]
    for target, out in zip(targets, (out_0, out_1, out_2, out_3)):
        for slot in range(3):
            i = jnp.clip(target - 1 + slot, 0, lats - 1)
            out[slot * tiles : (slot + 1) * tiles] = done[i]


def assemble_kernel(packed, from_core, from_cross, far, second, relay, ready):
    lat, lon, core = place()
    lats, lon_count = packed.shape
    edge = lats * STEPS
    width = lon_count // lax.axis_size("lon")
    blocks = lon_count // width
    way = 2 * core - 1
    partner = lon ^ 1
    pieces = [
        (packed[...], lon),
        (from_core[edge:], partner),
        (from_cross[edge:], lon + way),
        (far[...], lon + 4),
        (second[...], lon + 2 * way),
        (relay[:lats], partner - way),
        (relay[lats : 2 * lats], partner + 4),
        (relay[2 * lats :], partner - 2 * way),
    ]
    group = lax.broadcasted_iota(jnp.int32, (lats, lon_count), 1) // width
    turned = []
    for piece, at in pieces:
        at = lax.rem(at + blocks, blocks)
        turned.append((pltpu.roll(piece, at * width, 1), group == at))
    fields = []
    for f in range(FIELDS):
        total = None
        for piece, mask in turned:
            back = piece if f == 0 else pltpu.roll(piece, lon_count - f * width, 1)
            part = jnp.where(mask, back, 0.0)
            total = part if total is None else total + part
        fields.append(total)
    for step in range(STEPS):
        west, east, south, north, here = weights(
            fields[step], fields[STEPS + step], fields[2 * STEPS]
        )
        for row in range(lats):
            near = north if row % 2 == 0 else south
            over = north if row == 1 else south
            for at, weight in enumerate((west, east, near, over, here)):
                line = weight[row : row + 1]
                if at == 3 and row in (0, 3):
                    line = jnp.zeros_like(line)
                ready[step, at, lat ^ row] = jnp.broadcast_to(line, (8, lon_count))


def second_kernel(ready, kept, in_0, in_1, in_2, in_3, out, held, result):
    lat, _, _ = place()
    lon_count = kept.shape[1]
    for source, block in zip(SOURCES, (in_1, in_2, in_3)):
        held[lat ^ entry(source, lat)] = block[...]
    values = [in_0[...]] + [held[slot] for slot in (1, 2, 3)]
    for step, slots in enumerate(((0, 1, 2, 3), (0, 1, 3), (0,))):
        new = list(values)
        for s in slots:
            west, east, near, over, here = (ready[step, at, s][None] for at in range(5))
            value = here * values[s] + near * values[s ^ 1] + over * values[s ^ 3]
            value += west * pltpu.roll(values[s], 1, 2)
            value += east * pltpu.roll(values[s], lon_count - 1, 2)
            new[s] = value
        values = new
    result[...] = values[0].reshape(result.shape)
    for i in range(out.shape[1]):
        slot = i - lat + 1
        inside = (slot >= 0) & (slot <= 2)
        keep = (kept[i : i + 1] > 0.0) & inside
        out[0, i] = jnp.where(keep, result[jnp.clip(slot, 0, 2)], 0.0)


def on_chip(*arrays):
    return [pltpu.with_memory_space_constraint(array, pltpu.VMEM) for array in arrays]


def call(kernel, out_shape, scratch_shapes, *arrays):
    return pl.pallas_call(
        kernel,
        out_shape=out_shape,
        in_specs=[VMEM] * len(arrays),
        out_specs=(VMEM,) * len(out_shape) if isinstance(out_shape, tuple) else VMEM,
        scratch_shapes=scratch_shapes,
    )(*on_chip(*arrays))


def single_row(covariance, winds, diffusivity, cutoff):
    _, lats, width, lon_count = covariance.shape
    count = lax.axis_size("lon")

    def shape(*dims):
        return pltpu.VMEM(dims, jnp.float32)

    edge = shape(lats * STEPS + lats, lon_count)
    wind = shape(lats, lon_count)
    tiles = width // 8
    message = shape(3 * tiles, 8, lon_count)
    square = shape(lon_count, lon_count)
    to_core, to_cross, packed, banded, kept = pl.pallas_call(
        prepare_kernel,
        out_shape=(edge, edge, wind, shape(lats, width, lon_count), wind),
        in_specs=[SMEM, VMEM, VMEM, VMEM],
        out_specs=(VMEM,) * 5,
    )(cutoff, covariance, winds, diffusivity)

    lons = range(count)
    pair = [(m, m ^ 1) for m in lons]
    way = [2 * (m % 2) - 1 for m in lons]
    from_cross = lax.ppermute(to_cross, "lon", [((m + way[m]) % count, m) for m in lons])
    from_core = lax.ppermute(to_core, "lon", pair)
    far = lax.ppermute(packed, "lon", [((m + 4) % count, m) for m in lons])
    second = lax.ppermute(packed, "lon", [((m + 2 * way[m]) % count, m) for m in lons])
    middle = call(middle_kernel, shape(STEPS, lats, 5, width, lon_count), [square], packed)

    outs = call(
        first_kernel,
        (message,) * 4,
        [square, shape(lats, tiles, 8, lon_count)],
        banded,
        middle,
        from_core,
        from_cross,
    )
    ins = [outs[0]]
    for at, to in enumerate(TARGETS, start=1):
        ins.append(lax.ppermute(outs[at], "lat", list(enumerate(to))))
    winds_here = jnp.concatenate([from_cross[lats * STEPS :], far, second])
    relay = lax.ppermute(winds_here, "lon", pair)
    ready = call(
        assemble_kernel,
        shape(STEPS, 5, lats, 8, lon_count),
        [],
        packed,
        from_core,
        from_cross,
        far,
        second,
        relay,
    )
    return call(
        second_kernel,
        jax.ShapeDtypeStruct(covariance.shape, jnp.float32),
        [shape(lats, 3 * tiles, 8, lon_count), shape(3, width, lon_count)],
        ready,
        kept,
        *ins,
    )


def per_device(covariance, winds, diffusivity, cutoff):
    fits = lax.axis_size("lat") == 4 and lax.axis_size("lon") == 8
    fits = fits and covariance.shape == (1, 4, 16, 128)
    return (single_row if fits else general)(covariance, winds, diffusivity, cutoff)


def solution(mesh):
    in_specs = (P("lat", None, "lon", None), P(None, None, None, "lon"), P(None, "lon"), P())
    out_specs = P("lat", None, "lon", None)
    return jax.shard_map(
        per_device, mesh=mesh, in_specs=in_specs, out_specs=out_specs, check_vma=False
    )
```

```python
import functools

import jax
import jax.numpy as jnp
from jax import lax
from jax.experimental import pallas as pl
from jax.experimental.pallas import tpu as pltpu
from jax.sharding import PartitionSpec as P

STEPS = 3
FIELDS = 2 * STEPS + 1
ROUTES = (
    (8, 9, 10, 11, 12, 13, 22, 14, 16, 17, 2, 27, 20, 21, 19, 31, 24, 25, 26, 23, 4, 5, 30, 7, 0, 1, 18, 3, 29, 28, 6, 15),
    (3, 17, 10, 19, 20, 29, 14, 23, 9, 25, 11, 15, 8, 12, 30, 6, 0, 1, 16, 27, 28, 13, 18, 22, 21, 24, 2, 26, 4, 5, 31, 7),
    (24, 25, 26, 27, 28, 21, 30, 15, 0, 1, 18, 19, 4, 5, 22, 7, 8, 20, 2, 3, 17, 29, 6, 31, 16, 9, 10, 11, 12, 13, 14, 23),
    (16, 0, 18, 2, 5, 4, 7, 31, 24, 1, 26, 3, 28, 29, 6, 23, 25, 9, 10, 11, 12, 13, 14, 15, 8, 17, 27, 19, 20, 21, 22, 30),
)
EXCHANGES = len(ROUTES)
VMEM = pl.BlockSpec(memory_space=pltpu.VMEM)


def shifted(shard, axis, by, wrap):
    size = lax.axis_size(axis)
    pairs = [(i, (i + by) % size) for i in range(size) if wrap or 0 <= i + by < size]
    return lax.ppermute(shard, axis, pairs)


def weights(east_wind, north_wind, spread):
    west = jnp.maximum(east_wind, 0.0) + spread
    east = spread - jnp.minimum(east_wind, 0.0)
    south = jnp.maximum(north_wind, 0.0) + spread
    north = spread - jnp.minimum(north_wind, 0.0)
    return west, east, south, north, 1.0 - (west + east + south + north)


def general(covariance, winds, diffusivity, cutoff):
    row_count, lat_count, lon_local, _ = covariance.shape
    blocks = lat_count // row_count
    device_index = lax.axis_index("lat")
    rows = device_index * row_count + jnp.arange(row_count, dtype=jnp.int32)
    lats = jnp.arange(lat_count, dtype=jnp.int32)
    keep = jnp.abs(lats[None, :] - rows[:, None]) <= cutoff[None, :]
    keep = keep[:, :, None, None]
    stacked = jnp.concatenate([winds.reshape(2 * STEPS, lat_count, lon_local), diffusivity[None]])
    everywhere = lax.all_gather(stacked, "lon", axis=2, tiled=True)
    left = shifted(stacked[:, :, -STEPS:], "lon", 1, True)
    right = shifted(stacked[:, :, :STEPS], "lon", -1, True)
    near = jnp.concatenate([left, stacked, right], axis=2)

    field = jnp.where(keep, covariance, 0.0)
    left = shifted(field[:, :, -STEPS:], "lon", 1, True)
    right = shifted(field[:, :, :STEPS], "lon", -1, True)
    field = jnp.concatenate([left, field, right], axis=2)
    for step in range(STEPS):
        width = near.shape[2] - 2 * step
        take = functools.partial(lax.slice_in_dim, start_index=step + 1, limit_index=step + width - 1, axis=1)
        west, east, south, north, own = (
            w[None, :, :, None]
            for w in weights(take(near[step]), take(near[STEPS + step]), take(near[2 * STEPS]))
        )
        center = field[:, :, 1:-1]
        none = jnp.zeros_like(center[:, :1])
        field = (
            own * center
            + west * field[:, :, :-2]
            + east * field[:, :, 2:]
            + south * jnp.concatenate([none, center[:, :-1]], axis=1)
            + north * jnp.concatenate([center[:, 1:], none], axis=1)
        )

    reach = min(-(-STEPS // row_count), blocks - 1)
    halo = min(STEPS, reach * row_count)
    below = [shifted(field, "lat", by, False) for by in range(reach, 0, -1)]
    above = [shifted(field, "lat", -by, False) for by in range(1, reach + 1)]
    window = jnp.concatenate([*below, field, *above])
    window = window[reach * row_count - halo : (reach + 1) * row_count + halo]
    padded = jnp.pad(everywhere, ((0, 0), (halo, halo), (0, 0)))
    local = lax.dynamic_slice_in_dim(padded, device_index * row_count, row_count + 2 * halo, 1)
    for step in range(STEPS):
        west, east, south, north, own = (
            w[:, None, None, :] for w in weights(local[step], local[STEPS + step], local[2 * STEPS])
        )
        none = jnp.zeros_like(window[:1])
        window = (
            own * window
            + west * jnp.roll(window, 1, axis=3)
            + east * jnp.roll(window, -1, axis=3)
            + south * jnp.concatenate([none, window[:-1]])
            + north * jnp.concatenate([window[1:], none])
        )
        inside = device_index * row_count - halo + jnp.arange(window.shape[0])
        inside = (inside >= 0) & (inside < lat_count)
        window = jnp.where(inside[:, None, None, None], window, 0.0)
    return jnp.where(keep, window[halo : halo + row_count], 0.0)


def place():
    lon = lax.axis_index("lon")
    return lax.axis_index("lat"), lon, lax.rem(lon, 2)


def packed_rows(at, coming, first, blocks):
    route, rows, word = ROUTES[at], 4, 0
    for block in range(first, first + 4):
        for row in range(rows):
            device = blocks * row + block
            other = route.index(device) if coming else route[device]
            same = other % blocks == block
            word |= (other // blocks if same else row) << 2 * (rows * (block - first) + row)
    return jnp.int32(word - (1 << 32) if word >> 31 else word)


def rows_here(coming):
    lat, lon, _ = place()
    blocks = lax.axis_size("lon")
    at = 2 * (4 * (lon & 3) + lat)
    words = [
        jnp.where(lon < 4, *(packed_rows(step, coming, first, blocks) for first in (0, 4)))
        for step in range(EXCHANGES)
    ]
    return [lax.shift_right_logical(word, at) & 3 for word in words]


def prepare_kernel(
    cutoff_in,
    covariance_in,
    winds_in,
    diffusivity_in,
    to_core,
    to_cross,
    packed,
    banded,
    kept,
    cutoff,
    covariance,
    winds,
    diffusivity,
    arrived,
):
    copies = [
        pltpu.make_async_copy(source, target, arrived.at[at])
        for at, (source, target) in enumerate(
            (
                (winds_in, winds),
                (diffusivity_in, diffusivity),
                (covariance_in, covariance),
                (cutoff_in, cutoff),
            )
        )
    ]
    for copy in copies:
        copy.start()
    lat, _, core = place()
    lats, width, lon_count = banded.shape
    packed[...] = jnp.zeros_like(packed)
    copies[0].wait()
    copies[1].wait()
    for step in range(STEPS):
        for kind in range(2):
            at = (kind * STEPS + step) * width
            packed[:, at : at + width] = winds[kind, step]
    packed[:, 2 * STEPS * width : FIELDS * width] = diffusivity[...]
    rows = pl.ds(lats * STEPS, lats)
    to_core[rows] = packed[...]
    to_cross[rows] = packed[...]
    copies[2].wait()
    copies[3].wait()
    for i in range(lats):
        keep = jnp.abs(i - lat) <= cutoff[i]
        kept[i : i + 1] = jnp.full((1, lon_count), jnp.where(keep, 1.0, 0.0), jnp.float32)
        banded[i] = jnp.where(keep, covariance[0, i], 0.0)
        first, last = banded[i, :STEPS], banded[i, width - STEPS :]
        rows = pl.ds(i * STEPS, STEPS)
        to_core[rows] = jnp.where(core == 0, last, first)
        to_cross[rows] = jnp.where(core == 0, first, last)


def turn(*pieces):
    return jnp.concatenate(pieces).T


def middle_kernel(packed, middle):
    lats, lon_count = packed.shape
    width = middle.shape[3]
    turned = turn(packed[...], packed[...])

    def column(f, i):
        return jnp.broadcast_to(turned[f * width : (f + 1) * width, i : i + 1], (width, lon_count))

    for i in range(lats):
        spread = column(2 * STEPS, i)
        for step in range(STEPS):
            found = weights(column(step, i), column(STEPS + step, i), spread)
            for at, weight in enumerate(found):
                middle[step, i, at] = weight


def first_kernel(banded, middle, from_core, from_cross, *outs_and_done):
    *outs, done = outs_and_done
    lat, _, core = place()
    lats, width, lon_count = banded.shape
    edge = lats * STEPS
    left = jnp.where(core == 0, from_cross[...], from_core[...])
    right = jnp.where(core == 0, from_core[...], from_cross[...])
    turned = turn(left[edge:], right[edge:])

    def column(f, i):
        low = turned[(f + 1) * width - 8 : (f + 1) * width, i : i + 1]
        high = turned[f * width : f * width + 8, lats + i : lats + i + 1]
        return jnp.broadcast_to(jnp.concatenate([low, high]), (16, lon_count))

    gap = jnp.zeros((8 - STEPS, lon_count), jnp.float32)
    field = []
    for i in range(lats):
        rows = slice(i * STEPS, (i + 1) * STEPS)
        field.append(jnp.concatenate([gap, left[rows], banded[i], right[rows], gap]))
    spread = [column(2 * STEPS, i) for i in range(lats)]
    for step in range(STEPS):
        new = []
        for i in range(lats):
            outer = weights(column(step, i), column(STEPS + step, i), spread[i])
            west, east, south, north, here = (
                jnp.concatenate([w[:8], middle[step, i, at], w[8:]]) for at, w in enumerate(outer)
            )
            value = here * field[i]
            value += west * pltpu.roll(field[i], 1, 0)
            value += east * pltpu.roll(field[i], width + 15, 0)
            if i > 0:
                value += south * field[i - 1]
            if i < lats - 1:
                value += north * field[i + 1]
            new.append(value)
        field = new
    for i in range(lats):
        done[i] = field[i][8 : 8 + width].reshape(done.shape[1:])
    tiles = width // 8
    for target, out in zip([lat] + rows_here(False), outs):
        for slot in range(3):
            i = jnp.clip(target - 1 + slot, 0, lats - 1)
            out[slot * tiles : (slot + 1) * tiles] = done[i]


def assemble_kernel(packed, from_core, from_cross, far, second, relay, ready):
    lat, lon, core = place()
    lats, lon_count = packed.shape
    edge = lats * STEPS
    width = lon_count // lax.axis_size("lon")
    blocks = lon_count // width
    way = 2 * core - 1
    partner = lon ^ 1
    pieces = [
        (packed[...], lon),
        (from_core[edge:], partner),
        (from_cross[edge:], lon + way),
        (far[...], lon + 4),
        (second[...], lon + 2 * way),
        (relay[:lats], partner - way),
        (relay[lats : 2 * lats], partner + 4),
        (relay[2 * lats :], partner - 2 * way),
    ]
    group = lax.broadcasted_iota(jnp.int32, (lats, lon_count), 1) // width
    turned = []
    for piece, at in pieces:
        at = lax.rem(at + blocks, blocks)
        turned.append((pltpu.roll(piece, at * width, 1), group == at))
    fields = []
    for f in range(FIELDS):
        total = None
        for piece, mask in turned:
            back = piece if f == 0 else pltpu.roll(piece, lon_count - f * width, 1)
            part = jnp.where(mask, back, 0.0)
            total = part if total is None else total + part
        fields.append(total)
    for step in range(STEPS):
        west, east, south, north, here = weights(
            fields[step], fields[STEPS + step], fields[2 * STEPS]
        )
        for row in range(lats):
            near = north if row % 2 == 0 else south
            over = north if row == 1 else south
            for at, weight in enumerate((west, east, near, over, here)):
                line = weight[row : row + 1]
                if at == 3 and row in (0, 3):
                    line = jnp.zeros_like(line)
                ready[step, at, lat ^ row] = jnp.broadcast_to(line, (8, lon_count))


def second_kernel(ready, kept, own, *ins_and_rest):
    *ins, out, held, result = ins_and_rest
    lat, _, _ = place()
    lon_count = kept.shape[1]
    for row, block in zip(rows_here(True), ins):
        held[lat ^ row] = block[...]
    values = [own[...]] + [held[slot] for slot in (1, 2, 3)]
    for step, slots in enumerate(((0, 1, 2, 3), (0, 1, 3), (0,))):
        new = list(values)
        for s in slots:
            west, east, near, over, here = (ready[step, at, s][None] for at in range(5))
            value = here * values[s] + near * values[s ^ 1] + over * values[s ^ 3]
            value += west * pltpu.roll(values[s], 1, 2)
            value += east * pltpu.roll(values[s], lon_count - 1, 2)
            new[s] = value
        values = new
    result[...] = values[0].reshape(result.shape)
    for i in range(out.shape[1]):
        slot = i - lat + 1
        inside = (slot >= 0) & (slot <= 2)
        keep = (kept[i : i + 1] > 0.0) & inside
        out[0, i] = jnp.where(keep, result[jnp.clip(slot, 0, 2)], 0.0)


def on_chip(*arrays):
    return [pltpu.with_memory_space_constraint(array, pltpu.VMEM) for array in arrays]


def call(kernel, out_shape, scratch_shapes, *arrays):
    return pl.pallas_call(
        kernel,
        out_shape=out_shape,
        in_specs=[VMEM] * len(arrays),
        out_specs=(VMEM,) * len(out_shape) if isinstance(out_shape, tuple) else VMEM,
        scratch_shapes=scratch_shapes,
    )(*on_chip(*arrays))


def single_row(covariance, winds, diffusivity, cutoff):
    _, lats, width, lon_count = covariance.shape
    count = lax.axis_size("lon")

    def shape(*dims):
        return pltpu.VMEM(dims, jnp.float32)

    edge = shape(lats * STEPS + lats, lon_count)
    wind = shape(lats, lon_count)
    tiles = width // 8
    message = shape(3 * tiles, 8, lon_count)
    to_core, to_cross, packed, banded, kept = pl.pallas_call(
        prepare_kernel,
        out_shape=(edge, edge, wind, shape(lats, width, lon_count), wind),
        in_specs=[pl.BlockSpec(memory_space=pl.ANY)] * 4,
        out_specs=(VMEM,) * 5,
        scratch_shapes=[
            pltpu.SMEM(cutoff.shape, jnp.int32),
            shape(*covariance.shape),
            shape(*winds.shape),
            shape(*diffusivity.shape),
            pltpu.SemaphoreType.DMA((4,)),
        ],
    )(cutoff, covariance, winds, diffusivity)

    lons = range(count)
    pair = [(m, m ^ 1) for m in lons]
    way = [2 * (m % 2) - 1 for m in lons]
    from_cross = lax.ppermute(to_cross, "lon", [((m + way[m]) % count, m) for m in lons])
    from_core = lax.ppermute(to_core, "lon", pair)
    far = lax.ppermute(packed, "lon", [((m + 4) % count, m) for m in lons])
    second = lax.ppermute(packed, "lon", [((m + 2 * way[m]) % count, m) for m in lons])
    middle = call(middle_kernel, shape(STEPS, lats, 5, width, lon_count), [], packed)

    outs = call(
        first_kernel,
        (message,) * (1 + EXCHANGES),
        [shape(lats, tiles, 8, lon_count)],
        banded,
        middle,
        from_core,
        from_cross,
    )
    ins = [outs[0]]
    for at in range(EXCHANGES):
        pairs = list(enumerate(ROUTES[at]))
        ins.append(lax.ppermute(outs[1 + at], ("lat", "lon"), pairs))
    winds_here = jnp.concatenate([from_cross[lats * STEPS :], far, second])
    relay = lax.ppermute(winds_here, "lon", pair)
    ready = call(
        assemble_kernel,
        shape(STEPS, 5, lats, 8, lon_count),
        [],
        packed,
        from_core,
        from_cross,
        far,
        second,
        relay,
    )
    return call(
        second_kernel,
        jax.ShapeDtypeStruct(covariance.shape, jnp.float32),
        [shape(lats, 3 * tiles, 8, lon_count), shape(3, width, lon_count)],
        ready,
        kept,
        *ins,
    )


def per_device(covariance, winds, diffusivity, cutoff):
    fits = lax.axis_size("lat") == 4 and lax.axis_size("lon") == 8
    fits = fits and covariance.shape == (1, 4, 16, 128)
    return (single_row if fits else general)(covariance, winds, diffusivity, cutoff)


def solution(mesh):
    in_specs = (P("lat", None, "lon", None), P(None, None, None, "lon"), P(None, "lon"), P())
    out_specs = P("lat", None, "lon", None)
    return jax.shard_map(
        per_device, mesh=mesh, in_specs=in_specs, out_specs=out_specs, check_vma=False
    )
```

```python
import functools

import jax
import jax.numpy as jnp
from jax import lax
from jax.experimental import pallas as pl
from jax.experimental.pallas import tpu as pltpu
from jax.sharding import PartitionSpec as P

STEPS = 3
FIELDS = 2 * STEPS + 1
ROUTES = (
    (8, 9, 10, 11, 12, 13, 22, 14, 16, 17, 2, 27, 20, 21, 19, 31, 24, 25, 26, 23, 4, 5, 30, 7, 0, 1, 18, 3, 29, 28, 6, 15),
    (3, 17, 10, 19, 20, 29, 14, 23, 9, 25, 11, 15, 8, 12, 30, 6, 0, 1, 16, 27, 28, 13, 18, 22, 21, 24, 2, 26, 4, 5, 31, 7),
    (24, 25, 26, 27, 28, 21, 30, 15, 0, 1, 18, 19, 4, 5, 22, 7, 8, 20, 2, 3, 17, 29, 6, 31, 16, 9, 10, 11, 12, 13, 14, 23),
    (16, 0, 18, 2, 5, 4, 7, 31, 24, 1, 26, 3, 28, 29, 6, 23, 25, 9, 10, 11, 12, 13, 14, 15, 8, 17, 27, 19, 20, 21, 22, 30),
)
EXCHANGES = len(ROUTES)
VMEM = pl.BlockSpec(memory_space=pltpu.VMEM)


def shifted(shard, axis, by, wrap):
    size = lax.axis_size(axis)
    pairs = [(i, (i + by) % size) for i in range(size) if wrap or 0 <= i + by < size]
    return lax.ppermute(shard, axis, pairs)


def weights(east_wind, north_wind, spread):
    west = jnp.maximum(east_wind, 0.0) + spread
    east = spread - jnp.minimum(east_wind, 0.0)
    south = jnp.maximum(north_wind, 0.0) + spread
    north = spread - jnp.minimum(north_wind, 0.0)
    return west, east, south, north, 1.0 - (west + east + south + north)


def general(covariance, winds, diffusivity, cutoff):
    row_count, lat_count, lon_local, _ = covariance.shape
    blocks = lat_count // row_count
    device_index = lax.axis_index("lat")
    rows = device_index * row_count + jnp.arange(row_count, dtype=jnp.int32)
    lats = jnp.arange(lat_count, dtype=jnp.int32)
    keep = jnp.abs(lats[None, :] - rows[:, None]) <= cutoff[None, :]
    keep = keep[:, :, None, None]
    stacked = jnp.concatenate([winds.reshape(2 * STEPS, lat_count, lon_local), diffusivity[None]])
    everywhere = lax.all_gather(stacked, "lon", axis=2, tiled=True)
    left = shifted(stacked[:, :, -STEPS:], "lon", 1, True)
    right = shifted(stacked[:, :, :STEPS], "lon", -1, True)
    near = jnp.concatenate([left, stacked, right], axis=2)

    field = jnp.where(keep, covariance, 0.0)
    left = shifted(field[:, :, -STEPS:], "lon", 1, True)
    right = shifted(field[:, :, :STEPS], "lon", -1, True)
    field = jnp.concatenate([left, field, right], axis=2)
    for step in range(STEPS):
        width = near.shape[2] - 2 * step
        take = functools.partial(lax.slice_in_dim, start_index=step + 1, limit_index=step + width - 1, axis=1)
        west, east, south, north, own = (
            w[None, :, :, None]
            for w in weights(take(near[step]), take(near[STEPS + step]), take(near[2 * STEPS]))
        )
        center = field[:, :, 1:-1]
        none = jnp.zeros_like(center[:, :1])
        field = (
            own * center
            + west * field[:, :, :-2]
            + east * field[:, :, 2:]
            + south * jnp.concatenate([none, center[:, :-1]], axis=1)
            + north * jnp.concatenate([center[:, 1:], none], axis=1)
        )

    reach = min(-(-STEPS // row_count), blocks - 1)
    halo = min(STEPS, reach * row_count)
    below = [shifted(field, "lat", by, False) for by in range(reach, 0, -1)]
    above = [shifted(field, "lat", -by, False) for by in range(1, reach + 1)]
    window = jnp.concatenate([*below, field, *above])
    window = window[reach * row_count - halo : (reach + 1) * row_count + halo]
    padded = jnp.pad(everywhere, ((0, 0), (halo, halo), (0, 0)))
    local = lax.dynamic_slice_in_dim(padded, device_index * row_count, row_count + 2 * halo, 1)
    for step in range(STEPS):
        west, east, south, north, own = (
            w[:, None, None, :] for w in weights(local[step], local[STEPS + step], local[2 * STEPS])
        )
        none = jnp.zeros_like(window[:1])
        window = (
            own * window
            + west * jnp.roll(window, 1, axis=3)
            + east * jnp.roll(window, -1, axis=3)
            + south * jnp.concatenate([none, window[:-1]])
            + north * jnp.concatenate([window[1:], none])
        )
        inside = device_index * row_count - halo + jnp.arange(window.shape[0])
        inside = (inside >= 0) & (inside < lat_count)
        window = jnp.where(inside[:, None, None, None], window, 0.0)
    return jnp.where(keep, window[halo : halo + row_count], 0.0)


def place():
    lon = lax.axis_index("lon")
    return lax.axis_index("lat"), lon, lax.rem(lon, 2)


def packed_rows(at, coming, first, blocks):
    route, rows, word = ROUTES[at], 4, 0
    for block in range(first, first + 4):
        for row in range(rows):
            device = blocks * row + block
            other = route.index(device) if coming else route[device]
            same = other % blocks == block
            word |= (other // blocks if same else row) << 2 * (rows * (block - first) + row)
    return jnp.int32(word - (1 << 32) if word >> 31 else word)


def rows_here(coming):
    lat, lon, _ = place()
    blocks = lax.axis_size("lon")
    at = 2 * (4 * (lon & 3) + lat)
    words = [
        jnp.where(lon < 4, *(packed_rows(step, coming, first, blocks) for first in (0, 4)))
        for step in range(EXCHANGES)
    ]
    return [lax.shift_right_logical(word, at) & 3 for word in words]


def prepare_kernel(
    cutoff_in,
    covariance_in,
    winds_in,
    diffusivity_in,
    to_core,
    to_cross,
    packed,
    banded,
    kept,
    cutoff,
    covariance,
    winds,
    diffusivity,
    lines,
    arrived,
):
    copies = [
        pltpu.make_async_copy(source, target, arrived.at[at])
        for at, (source, target) in enumerate(
            (
                (winds_in, winds),
                (diffusivity_in, diffusivity),
                (covariance_in, covariance),
                (cutoff_in, cutoff),
            )
        )
    ]
    for copy in copies:
        copy.start()
    lat, _, core = place()
    lats, width, lon_count = banded.shape
    packed[...] = jnp.zeros_like(packed)
    copies[0].wait()
    copies[1].wait()
    for step in range(STEPS):
        for kind in range(2):
            at = (kind * STEPS + step) * width
            packed[:, at : at + width] = winds[kind, step]
    packed[:, 2 * STEPS * width : FIELDS * width] = diffusivity[...]
    rows = pl.ds(lats * STEPS, lats)
    to_core[rows] = packed[...]
    to_cross[rows] = packed[...]
    lines[...] = jnp.zeros_like(lines)
    for step in range(STEPS):
        for kind in range(2):
            at = (kind * STEPS + step) * lats
            lines[at : at + lats, :width] = winds[kind, step]
    lines[2 * STEPS * lats : FIELDS * lats, :width] = diffusivity[...]
    turned = lines[...].T
    first, last = turned[:8], turned[width - 8 : width]
    past = lats * (STEPS + 1)
    to_core[past:] = jnp.where(core == 0, last, first)
    to_cross[past:] = jnp.where(core == 0, first, last)
    copies[2].wait()
    copies[3].wait()
    for i in range(lats):
        keep = jnp.abs(i - lat) <= cutoff[i]
        kept[i : i + 1] = jnp.full((1, lon_count), jnp.where(keep, 1.0, 0.0), jnp.float32)
        banded[i] = jnp.where(keep, covariance[0, i], 0.0)
        first, last = banded[i, :STEPS], banded[i, width - STEPS :]
        rows = pl.ds(i * STEPS, STEPS)
        to_core[rows] = jnp.where(core == 0, last, first)
        to_cross[rows] = jnp.where(core == 0, first, last)


def turn(*pieces):
    return jnp.concatenate(pieces).T


def middle_kernel(packed, middle):
    lats, lon_count = packed.shape
    width = middle.shape[3]
    turned = turn(packed[...], packed[...])

    def column(f, i):
        return jnp.broadcast_to(turned[f * width : (f + 1) * width, i : i + 1], (width, lon_count))

    for i in range(lats):
        spread = column(2 * STEPS, i)
        for step in range(STEPS):
            found = weights(column(step, i), column(STEPS + step, i), spread)
            for at, weight in enumerate(found):
                middle[step, i, at] = weight


def first_kernel(banded, middle, from_core, from_cross, *outs_and_done):
    *outs, done = outs_and_done
    lat, _, core = place()
    lats, width, lon_count = banded.shape
    edge = lats * STEPS
    left = jnp.where(core == 0, from_cross[...], from_core[...])
    right = jnp.where(core == 0, from_core[...], from_cross[...])
    past = edge + lats

    def column(f, i):
        low, high = (side[past:, f * lats + i : f * lats + i + 1] for side in (left, right))
        return jnp.broadcast_to(jnp.concatenate([low, high]), (16, lon_count))

    gap = jnp.zeros((8 - STEPS, lon_count), jnp.float32)
    field = []
    for i in range(lats):
        rows = slice(i * STEPS, (i + 1) * STEPS)
        field.append(jnp.concatenate([gap, left[rows], banded[i], right[rows], gap]))
    spread = [column(2 * STEPS, i) for i in range(lats)]
    for step in range(STEPS):
        new = []
        for i in range(lats):
            outer = weights(column(step, i), column(STEPS + step, i), spread[i])
            west, east, south, north, here = (
                jnp.concatenate([w[:8], middle[step, i, at], w[8:]]) for at, w in enumerate(outer)
            )
            value = here * field[i]
            value += west * pltpu.roll(field[i], 1, 0)
            value += east * pltpu.roll(field[i], width + 15, 0)
            if i > 0:
                value += south * field[i - 1]
            if i < lats - 1:
                value += north * field[i + 1]
            new.append(value)
        field = new
    for i in range(lats):
        done[i] = field[i][8 : 8 + width].reshape(done.shape[1:])
    tiles = width // 8
    for target, out in zip([lat] + rows_here(False), outs):
        for slot in range(3):
            i = jnp.clip(target - 1 + slot, 0, lats - 1)
            out[slot * tiles : (slot + 1) * tiles] = done[i]


def assemble_kernel(packed, from_core, from_cross, far, second, relay, ready):
    lat, lon, core = place()
    lats, lon_count = packed.shape
    edge = lats * STEPS
    width = lon_count // lax.axis_size("lon")
    blocks = lon_count // width
    way = 2 * core - 1
    partner = lon ^ 1
    pieces = [
        (packed[...], lon),
        (from_core[edge : edge + lats], partner),
        (from_cross[edge : edge + lats], lon + way),
        (far[...], lon + 4),
        (second[...], lon + 2 * way),
        (relay[:lats], partner - way),
        (relay[lats : 2 * lats], partner + 4),
        (relay[2 * lats :], partner - 2 * way),
    ]
    group = lax.broadcasted_iota(jnp.int32, (lats, lon_count), 1) // width
    turned = []
    for piece, at in pieces:
        at = lax.rem(at + blocks, blocks)
        turned.append((pltpu.roll(piece, at * width, 1), group == at))
    fields = []
    for f in range(FIELDS):
        total = None
        for piece, mask in turned:
            back = piece if f == 0 else pltpu.roll(piece, lon_count - f * width, 1)
            part = jnp.where(mask, back, 0.0)
            total = part if total is None else total + part
        fields.append(total)
    for step in range(STEPS):
        west, east, south, north, here = weights(
            fields[step], fields[STEPS + step], fields[2 * STEPS]
        )
        for row in range(lats):
            near = north if row % 2 == 0 else south
            over = north if row == 1 else south
            for at, weight in enumerate((west, east, near, over, here)):
                line = weight[row : row + 1]
                if at == 3 and row in (0, 3):
                    line = jnp.zeros_like(line)
                ready[step, at, lat ^ row] = jnp.broadcast_to(line, (8, lon_count))


def second_kernel(ready, kept, own, *ins_and_rest):
    *ins, out, held, result = ins_and_rest
    lat, _, _ = place()
    lon_count = kept.shape[1]
    for row, block in zip(rows_here(True), ins):
        held[lat ^ row] = block[...]
    values = [own[...]] + [held[slot] for slot in (1, 2, 3)]
    for step, slots in enumerate(((0, 1, 2, 3), (0, 1, 3), (0,))):
        new = list(values)
        for s in slots:
            west, east, near, over, here = (ready[step, at, s][None] for at in range(5))
            value = here * values[s] + near * values[s ^ 1] + over * values[s ^ 3]
            value += west * pltpu.roll(values[s], 1, 2)
            value += east * pltpu.roll(values[s], lon_count - 1, 2)
            new[s] = value
        values = new
    result[...] = values[0].reshape(result.shape)
    for i in range(out.shape[1]):
        slot = i - lat + 1
        inside = (slot >= 0) & (slot <= 2)
        keep = (kept[i : i + 1] > 0.0) & inside
        out[0, i] = jnp.where(keep, result[jnp.clip(slot, 0, 2)], 0.0)


def on_chip(*arrays):
    return [pltpu.with_memory_space_constraint(array, pltpu.VMEM) for array in arrays]


def call(kernel, out_shape, scratch_shapes, *arrays):
    return pl.pallas_call(
        kernel,
        out_shape=out_shape,
        in_specs=[VMEM] * len(arrays),
        out_specs=(VMEM,) * len(out_shape) if isinstance(out_shape, tuple) else VMEM,
        scratch_shapes=scratch_shapes,
    )(*on_chip(*arrays))


def single_row(covariance, winds, diffusivity, cutoff):
    _, lats, width, lon_count = covariance.shape
    count = lax.axis_size("lon")

    def shape(*dims):
        return pltpu.VMEM(dims, jnp.float32)

    edge = shape(lats * (STEPS + 1) + 8, lon_count)
    wind = shape(lats, lon_count)
    tiles = width // 8
    message = shape(3 * tiles, 8, lon_count)
    to_core, to_cross, packed, banded, kept = pl.pallas_call(
        prepare_kernel,
        out_shape=(edge, edge, wind, shape(lats, width, lon_count), wind),
        in_specs=[pl.BlockSpec(memory_space=pl.ANY)] * 4,
        out_specs=(VMEM,) * 5,
        scratch_shapes=[
            pltpu.SMEM(cutoff.shape, jnp.int32),
            shape(*covariance.shape),
            shape(*winds.shape),
            shape(*diffusivity.shape),
            shape(lon_count, lon_count),
            pltpu.SemaphoreType.DMA((4,)),
        ],
    )(cutoff, covariance, winds, diffusivity)

    lons = range(count)
    pair = [(m, m ^ 1) for m in lons]
    way = [2 * (m % 2) - 1 for m in lons]
    from_cross = lax.ppermute(to_cross, "lon", [((m + way[m]) % count, m) for m in lons])
    from_core = lax.ppermute(to_core, "lon", pair)
    far = lax.ppermute(packed, "lon", [((m + 4) % count, m) for m in lons])
    second = lax.ppermute(packed, "lon", [((m + 2 * way[m]) % count, m) for m in lons])
    middle = call(middle_kernel, shape(STEPS, lats, 5, width, lon_count), [], packed)

    outs = call(
        first_kernel,
        (message,) * (1 + EXCHANGES),
        [shape(lats, tiles, 8, lon_count)],
        banded,
        middle,
        from_core,
        from_cross,
    )
    ins = [outs[0]]
    for at in range(EXCHANGES):
        pairs = list(enumerate(ROUTES[at]))
        ins.append(lax.ppermute(outs[1 + at], ("lat", "lon"), pairs))
    winds_here = jnp.concatenate(
        [from_cross[lats * STEPS : lats * (STEPS + 1)], far, second]
    )
    relay = lax.ppermute(winds_here, "lon", pair)
    ready = call(
        assemble_kernel,
        shape(STEPS, 5, lats, 8, lon_count),
        [],
        packed,
        from_core,
        from_cross,
        far,
        second,
        relay,
    )
    return call(
        second_kernel,
        jax.ShapeDtypeStruct(covariance.shape, jnp.float32),
        [shape(lats, 3 * tiles, 8, lon_count), shape(3, width, lon_count)],
        ready,
        kept,
        *ins,
    )


def per_device(covariance, winds, diffusivity, cutoff):
    fits = lax.axis_size("lat") == 4 and lax.axis_size("lon") == 8
    fits = fits and covariance.shape == (1, 4, 16, 128)
    return (single_row if fits else general)(covariance, winds, diffusivity, cutoff)


def solution(mesh):
    in_specs = (P("lat", None, "lon", None), P(None, None, None, "lon"), P(None, "lon"), P())
    out_specs = P("lat", None, "lon", None)
    return jax.shard_map(
        per_device, mesh=mesh, in_specs=in_specs, out_specs=out_specs, check_vma=False
    )
```

```python
import functools

import jax
import jax.numpy as jnp
from jax import lax
from jax.experimental import pallas as pl
from jax.experimental.pallas import tpu as pltpu
from jax.sharding import PartitionSpec as P

STEPS = 3
FIELDS = 2 * STEPS + 1
ROUTES = (
    (8, 9, 10, 11, 12, 13, 22, 14, 16, 17, 2, 27, 20, 21, 19, 31, 24, 25, 26, 23, 4, 5, 30, 7, 0, 1, 18, 3, 29, 28, 6, 15),
    (3, 17, 10, 19, 20, 29, 14, 23, 9, 25, 11, 15, 8, 12, 30, 6, 0, 1, 16, 27, 28, 13, 18, 22, 21, 24, 2, 26, 4, 5, 31, 7),
    (24, 25, 26, 27, 28, 21, 30, 15, 0, 1, 18, 19, 4, 5, 22, 7, 8, 20, 2, 3, 17, 29, 6, 31, 16, 9, 10, 11, 12, 13, 14, 23),
    (16, 0, 18, 2, 5, 4, 7, 31, 24, 1, 26, 3, 28, 29, 6, 23, 25, 9, 10, 11, 12, 13, 14, 15, 8, 17, 27, 19, 20, 21, 22, 30),
)
EXCHANGES = len(ROUTES)
VMEM = pl.BlockSpec(memory_space=pltpu.VMEM)


def shifted(shard, axis, by, wrap):
    size = lax.axis_size(axis)
    pairs = [(i, (i + by) % size) for i in range(size) if wrap or 0 <= i + by < size]
    return lax.ppermute(shard, axis, pairs)


def weights(east_wind, north_wind, spread):
    west = jnp.maximum(east_wind, 0.0) + spread
    east = spread - jnp.minimum(east_wind, 0.0)
    south = jnp.maximum(north_wind, 0.0) + spread
    north = spread - jnp.minimum(north_wind, 0.0)
    return west, east, south, north, 1.0 - (west + east + south + north)


def general(covariance, winds, diffusivity, cutoff):
    row_count, lat_count, lon_local, _ = covariance.shape
    blocks = lat_count // row_count
    device_index = lax.axis_index("lat")
    rows = device_index * row_count + jnp.arange(row_count, dtype=jnp.int32)
    lats = jnp.arange(lat_count, dtype=jnp.int32)
    keep = jnp.abs(lats[None, :] - rows[:, None]) <= cutoff[None, :]
    keep = keep[:, :, None, None]
    stacked = jnp.concatenate([winds.reshape(2 * STEPS, lat_count, lon_local), diffusivity[None]])
    everywhere = lax.all_gather(stacked, "lon", axis=2, tiled=True)
    left = shifted(stacked[:, :, -STEPS:], "lon", 1, True)
    right = shifted(stacked[:, :, :STEPS], "lon", -1, True)
    near = jnp.concatenate([left, stacked, right], axis=2)

    field = jnp.where(keep, covariance, 0.0)
    left = shifted(field[:, :, -STEPS:], "lon", 1, True)
    right = shifted(field[:, :, :STEPS], "lon", -1, True)
    field = jnp.concatenate([left, field, right], axis=2)
    for step in range(STEPS):
        width = near.shape[2] - 2 * step
        take = functools.partial(lax.slice_in_dim, start_index=step + 1, limit_index=step + width - 1, axis=1)
        west, east, south, north, own = (
            w[None, :, :, None]
            for w in weights(take(near[step]), take(near[STEPS + step]), take(near[2 * STEPS]))
        )
        center = field[:, :, 1:-1]
        none = jnp.zeros_like(center[:, :1])
        field = (
            own * center
            + west * field[:, :, :-2]
            + east * field[:, :, 2:]
            + south * jnp.concatenate([none, center[:, :-1]], axis=1)
            + north * jnp.concatenate([center[:, 1:], none], axis=1)
        )

    reach = min(-(-STEPS // row_count), blocks - 1)
    halo = min(STEPS, reach * row_count)
    below = [shifted(field, "lat", by, False) for by in range(reach, 0, -1)]
    above = [shifted(field, "lat", -by, False) for by in range(1, reach + 1)]
    window = jnp.concatenate([*below, field, *above])
    window = window[reach * row_count - halo : (reach + 1) * row_count + halo]
    padded = jnp.pad(everywhere, ((0, 0), (halo, halo), (0, 0)))
    local = lax.dynamic_slice_in_dim(padded, device_index * row_count, row_count + 2 * halo, 1)
    for step in range(STEPS):
        west, east, south, north, own = (
            w[:, None, None, :] for w in weights(local[step], local[STEPS + step], local[2 * STEPS])
        )
        none = jnp.zeros_like(window[:1])
        window = (
            own * window
            + west * jnp.roll(window, 1, axis=3)
            + east * jnp.roll(window, -1, axis=3)
            + south * jnp.concatenate([none, window[:-1]])
            + north * jnp.concatenate([window[1:], none])
        )
        inside = device_index * row_count - halo + jnp.arange(window.shape[0])
        inside = (inside >= 0) & (inside < lat_count)
        window = jnp.where(inside[:, None, None, None], window, 0.0)
    return jnp.where(keep, window[halo : halo + row_count], 0.0)


def place():
    lon = lax.axis_index("lon")
    return lax.axis_index("lat"), lon, lax.rem(lon, 2)


def packed_rows(at, coming, first, blocks):
    route, rows, word = ROUTES[at], 4, 0
    for block in range(first, first + 4):
        for row in range(rows):
            device = blocks * row + block
            other = route.index(device) if coming else route[device]
            same = other % blocks == block
            word |= (other // blocks if same else row) << 2 * (rows * (block - first) + row)
    return jnp.int32(word - (1 << 32) if word >> 31 else word)


def rows_here(coming):
    lat, lon, _ = place()
    blocks = lax.axis_size("lon")
    at = 2 * (4 * (lon & 3) + lat)
    words = [
        jnp.where(lon < 4, *(packed_rows(step, coming, first, blocks) for first in (0, 4)))
        for step in range(EXCHANGES)
    ]
    return [lax.shift_right_logical(word, at) & 3 for word in words]


def prepare_kernel(
    cutoff_in,
    covariance_in,
    winds_in,
    diffusivity_in,
    to_core,
    to_cross,
    packed,
    banded,
    kept,
    upright,
    cutoff,
    covariance,
    winds,
    diffusivity,
    lines,
    arrived,
):
    copies = [
        pltpu.make_async_copy(source, target, arrived.at[at])
        for at, (source, target) in enumerate(
            (
                (winds_in, winds),
                (diffusivity_in, diffusivity),
                (covariance_in, covariance),
                (cutoff_in, cutoff),
            )
        )
    ]
    for copy in copies:
        copy.start()
    lat, _, core = place()
    lats, width, lon_count = banded.shape
    packed[...] = jnp.zeros_like(packed)
    copies[0].wait()
    copies[1].wait()
    for step in range(STEPS):
        for kind in range(2):
            at = (kind * STEPS + step) * width
            packed[:, at : at + width] = winds[kind, step]
    packed[:, 2 * STEPS * width : FIELDS * width] = diffusivity[...]
    rows = pl.ds(lats * STEPS, lats)
    to_core[rows] = packed[...]
    to_cross[rows] = packed[...]
    lines[...] = jnp.zeros_like(lines)
    for step in range(STEPS):
        for kind in range(2):
            at = (kind * STEPS + step) * lats
            lines[at : at + lats, :width] = winds[kind, step]
    lines[2 * STEPS * lats : FIELDS * lats, :width] = diffusivity[...]
    turned = lines[...].T
    first, last = turned[:8], turned[width - 8 : width]
    upright[...] = turned[:width]
    past = lats * (STEPS + 1)
    to_core[past:] = jnp.where(core == 0, last, first)
    to_cross[past:] = jnp.where(core == 0, first, last)
    copies[2].wait()
    copies[3].wait()
    for i in range(lats):
        keep = jnp.abs(i - lat) <= cutoff[i]
        kept[i : i + 1] = jnp.full((1, lon_count), jnp.where(keep, 1.0, 0.0), jnp.float32)
        banded[i] = jnp.where(keep, covariance[0, i], 0.0)
        first, last = banded[i, :STEPS], banded[i, width - STEPS :]
        rows = pl.ds(i * STEPS, STEPS)
        to_core[rows] = jnp.where(core == 0, last, first)
        to_cross[rows] = jnp.where(core == 0, first, last)


def middle_kernel(upright, middle):
    width, lon_count = upright.shape
    lats = middle.shape[1]

    def column(f, i):
        at = f * lats + i
        return jnp.broadcast_to(upright[:, at : at + 1], (width, lon_count))

    for i in range(lats):
        spread = column(2 * STEPS, i)
        for step in range(STEPS):
            found = weights(column(step, i), column(STEPS + step, i), spread)
            for at, weight in enumerate(found):
                middle[step, i, at] = weight


def first_kernel(banded, middle, from_core, from_cross, *outs_and_done):
    *outs, done = outs_and_done
    lat, _, core = place()
    lats, width, lon_count = banded.shape
    edge = lats * STEPS
    left = jnp.where(core == 0, from_cross[...], from_core[...])
    right = jnp.where(core == 0, from_core[...], from_cross[...])
    past = edge + lats

    def column(f, i):
        low, high = (side[past:, f * lats + i : f * lats + i + 1] for side in (left, right))
        return jnp.broadcast_to(jnp.concatenate([low, high]), (16, lon_count))

    gap = jnp.zeros((8 - STEPS, lon_count), jnp.float32)
    field = []
    for i in range(lats):
        rows = slice(i * STEPS, (i + 1) * STEPS)
        field.append(jnp.concatenate([gap, left[rows], banded[i], right[rows], gap]))
    spread = [column(2 * STEPS, i) for i in range(lats)]
    for step in range(STEPS):
        new = []
        for i in range(lats):
            outer = weights(column(step, i), column(STEPS + step, i), spread[i])
            west, east, south, north, here = (
                jnp.concatenate([w[:8], middle[step, i, at], w[8:]]) for at, w in enumerate(outer)
            )
            value = here * field[i]
            value += west * pltpu.roll(field[i], 1, 0)
            value += east * pltpu.roll(field[i], width + 15, 0)
            if i > 0:
                value += south * field[i - 1]
            if i < lats - 1:
                value += north * field[i + 1]
            new.append(value)
        field = new
    for i in range(lats):
        done[i] = field[i][8 : 8 + width].reshape(done.shape[1:])
    tiles = width // 8
    for target, out in zip([lat] + rows_here(False), outs):
        for slot in range(3):
            i = jnp.clip(target - 1 + slot, 0, lats - 1)
            out[slot * tiles : (slot + 1) * tiles] = done[i]


def assemble_kernel(packed, from_core, from_cross, far, second, relay, ready):
    lat, lon, core = place()
    lats, lon_count = packed.shape
    edge = lats * STEPS
    width = lon_count // lax.axis_size("lon")
    blocks = lon_count // width
    way = 2 * core - 1
    partner = lon ^ 1
    pieces = [
        (packed[...], lon),
        (from_core[edge : edge + lats], partner),
        (from_cross[edge : edge + lats], lon + way),
        (far[...], lon + 4),
        (second[...], lon + 2 * way),
        (relay[:lats], partner - way),
        (relay[lats : 2 * lats], partner + 4),
        (relay[2 * lats :], partner - 2 * way),
    ]
    group = lax.broadcasted_iota(jnp.int32, (lats, lon_count), 1) // width
    turned = []
    for piece, at in pieces:
        at = lax.rem(at + blocks, blocks)
        turned.append((pltpu.roll(piece, at * width, 1), group == at))
    fields = []
    for f in range(FIELDS):
        total = None
        for piece, mask in turned:
            back = piece if f == 0 else pltpu.roll(piece, lon_count - f * width, 1)
            part = jnp.where(mask, back, 0.0)
            total = part if total is None else total + part
        fields.append(total)
    for step in range(STEPS):
        west, east, south, north, here = weights(
            fields[step], fields[STEPS + step], fields[2 * STEPS]
        )
        for row in range(lats):
            near = north if row % 2 == 0 else south
            over = north if row == 1 else south
            for at, weight in enumerate((west, east, near, over, here)):
                line = weight[row : row + 1]
                if at == 3 and row in (0, 3):
                    line = jnp.zeros_like(line)
                ready[step, at, lat ^ row] = jnp.broadcast_to(line, (8, lon_count))


def second_kernel(ready, kept, own, *ins_and_rest):
    *ins, out, held, result = ins_and_rest
    lat, _, _ = place()
    lon_count = kept.shape[1]
    for row, block in zip(rows_here(True), ins):
        held[lat ^ row] = block[...]
    values = [own[...]] + [held[slot] for slot in (1, 2, 3)]
    for step, slots in enumerate(((0, 1, 2, 3), (0, 1, 3), (0,))):
        new = list(values)
        for s in slots:
            west, east, near, over, here = (ready[step, at, s][None] for at in range(5))
            value = here * values[s] + near * values[s ^ 1] + over * values[s ^ 3]
            value += west * pltpu.roll(values[s], 1, 2)
            value += east * pltpu.roll(values[s], lon_count - 1, 2)
            new[s] = value
        values = new
    result[...] = values[0].reshape(result.shape)
    for i in range(out.shape[1]):
        slot = i - lat + 1
        inside = (slot >= 0) & (slot <= 2)
        keep = (kept[i : i + 1] > 0.0) & inside
        out[0, i] = jnp.where(keep, result[jnp.clip(slot, 0, 2)], 0.0)


def on_chip(*arrays):
    return [pltpu.with_memory_space_constraint(array, pltpu.VMEM) for array in arrays]


def call(kernel, out_shape, scratch_shapes, *arrays):
    return pl.pallas_call(
        kernel,
        out_shape=out_shape,
        in_specs=[VMEM] * len(arrays),
        out_specs=(VMEM,) * len(out_shape) if isinstance(out_shape, tuple) else VMEM,
        scratch_shapes=scratch_shapes,
    )(*on_chip(*arrays))


def single_row(covariance, winds, diffusivity, cutoff):
    _, lats, width, lon_count = covariance.shape
    count = lax.axis_size("lon")

    def shape(*dims):
        return pltpu.VMEM(dims, jnp.float32)

    edge = shape(lats * (STEPS + 1) + 8, lon_count)
    wind = shape(lats, lon_count)
    tiles = width // 8
    message = shape(3 * tiles, 8, lon_count)
    to_core, to_cross, packed, banded, kept, upright = pl.pallas_call(
        prepare_kernel,
        out_shape=(edge, edge, wind, shape(lats, width, lon_count), wind, shape(width, lon_count)),
        in_specs=[pl.BlockSpec(memory_space=pl.ANY)] * 4,
        out_specs=(VMEM,) * 6,
        scratch_shapes=[
            pltpu.SMEM(cutoff.shape, jnp.int32),
            shape(*covariance.shape),
            shape(*winds.shape),
            shape(*diffusivity.shape),
            shape(lon_count, lon_count),
            pltpu.SemaphoreType.DMA((4,)),
        ],
    )(cutoff, covariance, winds, diffusivity)

    lons = range(count)
    pair = [(m, m ^ 1) for m in lons]
    way = [2 * (m % 2) - 1 for m in lons]
    from_cross = lax.ppermute(to_cross, "lon", [((m + way[m]) % count, m) for m in lons])
    from_core = lax.ppermute(to_core, "lon", pair)
    far = lax.ppermute(packed, "lon", [((m + 4) % count, m) for m in lons])
    second = lax.ppermute(packed, "lon", [((m + 2 * way[m]) % count, m) for m in lons])
    middle = call(middle_kernel, shape(STEPS, lats, 5, width, lon_count), [], upright)

    outs = call(
        first_kernel,
        (message,) * (1 + EXCHANGES),
        [shape(lats, tiles, 8, lon_count)],
        banded,
        middle,
        from_core,
        from_cross,
    )
    ins = [outs[0]]
    for at in range(EXCHANGES):
        pairs = list(enumerate(ROUTES[at]))
        ins.append(lax.ppermute(outs[1 + at], ("lat", "lon"), pairs))
    winds_here = jnp.concatenate(
        [from_cross[lats * STEPS : lats * (STEPS + 1)], far, second]
    )
    relay = lax.ppermute(winds_here, "lon", pair)
    ready = call(
        assemble_kernel,
        shape(STEPS, 5, lats, 8, lon_count),
        [],
        packed,
        from_core,
        from_cross,
        far,
        second,
        relay,
    )
    return call(
        second_kernel,
        jax.ShapeDtypeStruct(covariance.shape, jnp.float32),
        [shape(lats, 3 * tiles, 8, lon_count), shape(3, width, lon_count)],
        ready,
        kept,
        *ins,
    )


def per_device(covariance, winds, diffusivity, cutoff):
    fits = lax.axis_size("lat") == 4 and lax.axis_size("lon") == 8
    fits = fits and covariance.shape == (1, 4, 16, 128)
    return (single_row if fits else general)(covariance, winds, diffusivity, cutoff)


def solution(mesh):
    in_specs = (P("lat", None, "lon", None), P(None, None, None, "lon"), P(None, "lon"), P())
    out_specs = P("lat", None, "lon", None)
    return jax.shard_map(
        per_device, mesh=mesh, in_specs=in_specs, out_specs=out_specs, check_vma=False
    )
```
